512 devices in a mesh: gx: 8 (over z), gy: 8 (over x, core), gz: 8 (over y).
Axes of the slice: x: 4, y: 8, z: 8, core: 2. Of those that a mesh axis runs over, the one named last changes fastest.
Arguments:
- features: bfloat16 [8, 8, 8, 512, 128], P('gx', 'gy', 'gz'), may hold values from -6 to 6
- coords: float32 [8, 8, 8, 3, 512], P('gx', 'gy', 'gz'), as said below
- counts: int32 [8, 8, 8], P('gx', 'gy', 'gz'), may hold values from 128 to 512, as said below
- sources: int32 [8, 8, 8, 512], P('gx', 'gy', 'gz'), may hold values from 0 to 13823, as said below
- wanted: int32 [8, 8, 8, 2, 27, 1], P('gx', 'gy', 'gz'), may hold values from 0 to 7, as said below
- pairs: int32 [8, 8, 8, 2, 32], P('gx', 'gy', 'gz'), may hold values from 0 to 34, as said below
- lifting_weight: bfloat16 [2, 128, 128], replicated, may hold values from -0.5 to 0.5
- radial_weight: float32 [2, 3, 8, 128], replicated, may hold values from -2 to 2
- mix_weight: float32 [2, 3, 128], replicated, may hold values from -3 to 3
- out_weight: bfloat16 [2, 128, 128], replicated, may hold values from -0.5 to 0.5
- force_weight: float32 [8], replicated, may hold values from -4 to 4
Outputs:
- updated: bfloat16 [8, 8, 8, 512, 128], P('gx', 'gy', 'gz')
- forces: float32 [8, 8, 8, 3, 512], P('gx', 'gy', 'gz')
The draws below stay inside these ranges and needn't reach their ends.
Inputs may be any that keep to these rules, and one draw needn't show every extreme that they name: `counts`: some device holds exactly 512 live atoms. `sources`: the neighbour code of a value is value // 512 and its slot value % 512; every record of every device is taken by exactly one new slot. `wanted`: the 1 tiles read from one neighbour code in one layer are distinct. `pairs`: row 0 is below 8; a row 1 value v below 8 is an own tile, otherwise ghost slot (v - 8) % 1 of code (v - 8), never code 13. `coords`: each component lies in the cell, from 0 to 5120 ** (1/3), except for records taken by another device, which lie up to 1 outside the face toward their new owner.
All inputs are finite; a program needn't handle non-finite values.
Results may differ from the reference program's by a relative error of at most 0.0061.
Values may be sent and summed in bfloat16 or wider, within the bound.
A program may use at most 64 MiB of HBM per device.

```python
import math
import jax
import jax.numpy as jnp
import numpy as np
from jax import lax

C = 128
NB = 8
TILE = 64
LAYERS = 2
TILES = 8
GT = 1
PAIRS = 32
SLOTS = 512
N_GX = 8
N_GY = 8
N_GZ = 8


def migration_plan(key):
    slot_count = TILES * TILE
    slot_ids = jnp.arange(slot_count)
    within = slot_ids % TILE
    octant = slot_ids // TILE % 8
    octant_bits = (octant // 4, octant // 2 % 2, octant % 2)
    moving = jax.random.randint(jax.random.fold_in(key, 101), (slot_count,), 0, 8) == 0
    drawn_bits = jax.random.randint(jax.random.fold_in(key, 102), (slot_count,), 1, 8)
    picked = jnp.where(within < 7, within + 1, jnp.where(moving, drawn_bits, 0))
    offsets = (picked // 4 % 2 * (2 * octant_bits[0] - 1), picked // 2 % 2 * (2 * octant_bits[1] - 1), picked % 2 * (2 * octant_bits[2] - 1))
    direction_code = 9 * (offsets[0] + 1) + 3 * (offsets[1] + 1) + offsets[2] + 1
    shuffled = jax.random.permutation(jax.random.fold_in(key, 103), slot_count)
    return (direction_code, shuffled, offsets, octant_bits)


def draw_coords(key, part):
    direction_code, shuffled, offsets, octant_bits = migration_plan(key)
    slot_count = TILES * TILE
    cell_edge = (10.0 * slot_count) ** (1.0 / 3.0)
    half_edge = 0.5 * cell_edge
    uniform_draw = jax.random.uniform(jax.random.fold_in(key, 105), (N_GX, N_GY, N_GZ, 3, slot_count), jnp.float32)
    spread = uniform_draw
    axis_pieces_list = []
    for axis_number in range(3):
        high_side = (octant_bits[axis_number] == 1)[None, None, None, :]
        leaving = (offsets[axis_number] != 0)[None, None, None, :]
        drawn_draw = uniform_draw[:, :, :, axis_number]
        biased_draw = spread[:, :, :, axis_number]
        inner = jnp.where(high_side, half_edge + half_edge * biased_draw, half_edge - half_edge * biased_draw)
        near_face = jnp.where(high_side, cell_edge - drawn_draw, drawn_draw)
        axis_pieces_list.append(jnp.where(leaving, near_face, inner))
    placed = jnp.stack(axis_pieces_list, axis=3)
    by_base = jnp.zeros_like(placed)
    for code_number in range(27):
        step_x = code_number // 9 - 1
        step_y = code_number // 3 % 3 - 1
        step_z = code_number % 3 - 1
        rolled_rows = jnp.roll(placed, (step_x, step_y, step_z), axis=(0, 1, 2))
        shift_vector = jnp.array([step_x, step_y, step_z], jnp.float32) * cell_edge
        chosen = (direction_code == code_number)[None, None, None, None, :]
        by_base = jnp.where(chosen, rolled_rows - shift_vector[None, None, None, :, None], by_base)
    return jnp.zeros_like(by_base).at[:, :, :, :, shuffled].set(by_base)


def draw_counts(key, part):
    key_base, key_full = jax.random.split(key)
    devices = N_GX * N_GY * N_GZ
    slot_count = TILES * TILE
    base = jax.random.randint(key_base, (devices,), slot_count // 4, slot_count + 1)
    chosen_device = jax.random.randint(key_full, (), 0, devices)
    filled = jnp.where(jnp.arange(devices) == chosen_device, slot_count, base)
    return filled.reshape(N_GX, N_GY, N_GZ).astype(jnp.int32)


def draw_sources(key, part):
    direction_code, shuffled, offsets, octant_bits = migration_plan(key)
    slot_count = TILES * TILE
    devices = N_GX * N_GY * N_GZ

    def tile_order(subkey):
        return jax.random.permutation(subkey, TILE)
    orders = jax.vmap(tile_order)(jax.random.split(jax.random.fold_in(key, 104), devices * TILES))
    orders = (orders.reshape(devices, TILES, TILE) + (jnp.arange(TILES) * TILE)[None, :, None]).reshape(devices, slot_count)
    base = direction_code * slot_count + shuffled
    return base[orders].reshape(N_GX, N_GY, N_GZ, slot_count).astype(jnp.int32)


def draw_wanted(key, part):
    devices = N_GX * N_GY * N_GZ
    tile_ids = jnp.arange(TILES)
    tile_octant = tile_ids % 8
    code_ids = jnp.arange(27)
    allowed = jnp.ones((27, TILES), jnp.int32)
    for axis_number, divisor in ((0, 9), (1, 3), (2, 1)):
        code_step = code_ids // divisor % 3 - 1
        tile_bit = tile_octant // (4 // divisor if divisor > 1 else 1) % 2
        facing_bit = (1 - code_step) // 2
        fits = (code_step[:, None] == 0) | (tile_bit[None, :] == facing_bit[:, None])
        allowed = allowed * fits.astype(jnp.int32)

    def one_order(subkey):
        return jax.random.permutation(subkey, TILES)
    orders = jax.vmap(one_order)(jax.random.split(jax.random.fold_in(key, 201), devices * LAYERS * 27))
    orders = orders.reshape(devices, LAYERS, 27, TILES)
    scores = orders + TILES * allowed[None, None]
    picked = lax_top(scores)
    return picked.reshape(N_GX, N_GY, N_GZ, LAYERS, 27, GT).astype(jnp.int32)


def lax_top(scores):
    return jax.lax.top_k(scores, GT)[1]


def draw_pairs(key, part):
    pair_shape = (N_GX, N_GY, N_GZ, PAIRS)
    kind_draw = jax.random.randint(jax.random.fold_in(key, 301), pair_shape, 0, 2)
    own_target = jax.random.randint(jax.random.fold_in(key, 302), pair_shape, 0, TILES)
    own_source = jax.random.randint(jax.random.fold_in(key, 303), pair_shape, 0, TILES)
    drawn_code = jax.random.randint(jax.random.fold_in(key, 304), pair_shape, 0, 26)
    ghost_code = drawn_code + (drawn_code >= 13).astype(jnp.int32)
    ghost_slot = jax.random.randint(jax.random.fold_in(key, 305), pair_shape, 0, GT)
    free_bits = jax.random.randint(jax.random.fold_in(key, 306), pair_shape + (3,), 0, 2)
    group_pick = jax.random.randint(jax.random.fold_in(key, 307), pair_shape, 0, TILES // 8)
    octant_number = jnp.zeros(pair_shape, jnp.int32)
    for axis_number, divisor, weight_bit in ((0, 9, 4), (1, 3, 2), (2, 1, 1)):
        code_step = ghost_code // divisor % 3 - 1
        near_bit = jnp.where(code_step == 0, free_bits[..., axis_number], (code_step + 1) // 2)
        octant_number = octant_number + near_bit * weight_bit
    ghost_target = group_pick * 8 + octant_number
    ghost_source = TILES + ghost_code * GT + ghost_slot
    targets = jnp.where(kind_draw == 0, own_target, ghost_target)
    anchors = jnp.where(kind_draw == 0, own_source, ghost_source)
    return jnp.stack([targets, anchors], axis=3).astype(jnp.int32)


def block_levels(key, dims, cuts, least, top_value):
    def one(axis_at, parts):
        draws = jax.random.uniform(jax.random.fold_in(jax.random.fold_in(key, 6), axis_at), (parts,), jnp.float32, least / len(cuts), top_value / len(cuts))
        return jnp.repeat(jnp.exp(draws), dims[axis_at] // parts).reshape((-1,) + (1,) * (len(dims) - axis_at - 1))

    factor_of = one(*cuts[0])
    for cut in cuts[1:]:
        factor_of = factor_of * one(*cut)
    return factor_of


def normal_values(rng, shape, scale, reach, cuts=(), held_as=jnp.bfloat16):
    loudness = block_levels(rng, shape, cuts, -0.22, 0.18) if cuts else 1.0
    values = jax.random.normal(rng, shape, jnp.float32) * scale * loudness
    return jnp.minimum(jnp.maximum(values, -reach), reach).astype(held_as)


def setup_inputs(seed: int = 0) -> dict:
    splits = jax.random.split(jax.random.key(seed), 12)
    return {
        "features": normal_values(splits[0], (N_GX, N_GY, N_GZ, SLOTS, C), 1.0, 6.0, ((0, 8), (1, 8), (2, 8))),
        "coords": draw_coords(jax.random.fold_in(splits[11], 71), 0),
        "counts": draw_counts(jax.random.fold_in(splits[11], 71), 0),
        "sources": draw_sources(jax.random.fold_in(splits[11], 71), 0),
        "wanted": draw_wanted(jax.random.fold_in(splits[11], 71), 0),
        "pairs": draw_pairs(jax.random.fold_in(splits[11], 71), 0),
        "lifting_weight": normal_values(splits[6], (LAYERS, C, C), C ** -0.5, 0.5),
        "radial_weight": normal_values(splits[7], (LAYERS, 3, NB, C), 0.35, 2.0, (), jnp.float32),
        "mix_weight": normal_values(splits[8], (LAYERS, 3, C), 0.5, 3.0, (), jnp.float32),
        "out_weight": normal_values(splits[9], (LAYERS, C, C), C ** -0.5, 0.5),
        "force_weight": normal_values(splits[10], (NB,), 1.0, 4.0, (), jnp.float32),
    }


CUTOFF = 5.0
BASIS_WIDTH = 0.6
MESSAGE_SCALE = 0.2
SOFTENING = 0.25
FAR_AWAY = 1000.0
DEAD_SPACING = 100.0
DENSITY = 0.1

def offset_table():
    return np.array([[first_step, second_step, third_step] for first_step in (-1, 0, 1) for second_step in (-1, 0, 1) for third_step in (-1, 0, 1)], dtype=np.float32)

def harmonics(direction):
    along_x = direction[0]
    along_y = direction[1]
    along_z = direction[2]
    root_three = math.sqrt(3.0)
    root_five = math.sqrt(5.0)
    root_fifteen = math.sqrt(15.0)
    return jnp.stack([jnp.ones_like(along_x), root_three * along_x, root_three * along_y, root_three * along_z, root_fifteen * along_x * along_y, root_fifteen * along_y * along_z, 0.5 * root_five * (3.0 * along_z * along_z - 1.0), root_fifteen * along_x * along_z, 0.5 * root_fifteen * (along_x * along_x - along_y * along_y)])

def radial(distance):
    ratio = jnp.minimum(distance / CUTOFF, 1.0)
    envelope = (1.0 - ratio * ratio) ** 2
    centers = 0.5 + jnp.arange(NB).astype(jnp.float32) * (4.2 / (NB - 1))
    scaled = (distance[None] - centers[:, None, None]) / BASIS_WIDTH
    return jnp.exp(-scaled * scaled) * envelope[None]

def multiply(left, right):
    return jnp.dot(left.astype(jnp.float32), right.astype(jnp.float32), precision=lax.Precision.HIGHEST)

def pair_terms(place_i, place_j, rows_i, rows_j, same_tile, radial_layer, force_weight, with_force):
    tile_size = place_i.shape[1]
    channels = rows_j.shape[1]
    separation = place_i[:, :, None] - place_j[:, None, :]
    distance = jnp.sqrt(lax.optimization_barrier(jnp.sum(separation * separation, axis=0)) + SOFTENING)
    direction = separation / distance[None]
    keep_mask = 1.0 - same_tile * jnp.eye(tile_size, dtype=jnp.float32)
    basis = radial(distance) * keep_mask[None]
    angular = harmonics(direction)
    edges = (angular[:, :, None, :] * jnp.transpose(basis, (1, 0, 2))[None]).astype(jnp.bfloat16)
    edges = edges.reshape(9, tile_size, NB * tile_size)
    weighted = (radial_layer[:, :, None, :] * rows_j.astype(jnp.float32)[None, None]).astype(jnp.bfloat16)
    weighted = weighted.reshape(3, NB * tile_size, channels)
    groups = ((0, 1), (1, 4), (4, 9))
    pieces = []
    for degree in range(3):
        start_row, stop_row = groups[degree]
        edge_block = edges[start_row:stop_row].reshape((stop_row - start_row) * tile_size, NB * tile_size)
        pieces.append(multiply(edge_block, weighted[degree]).reshape(stop_row - start_row, tile_size, channels))
    message = jnp.concatenate(pieces, axis=0) * MESSAGE_SCALE
    if with_force:
        intersection = multiply(rows_i, rows_j.T) / math.sqrt(channels)
        profile = lax.optimization_barrier(jnp.sum(force_weight[:, None, None] * basis, axis=0))
        pushes = (profile * intersection)[None] * direction
        return (message, 0.5 * lax.optimization_barrier(jnp.sum(pushes, axis=2)), -0.5 * lax.optimization_barrier(jnp.sum(pushes, axis=1)))
    nothing = jnp.zeros((3, tile_size), jnp.float32)
    return (message, nothing, nothing)

def update(hidden_features, totals, mix_layer, out_layer):
    channels = hidden_features.shape[1]
    scalar_part = totals[:, 0]
    vector_part = lax.optimization_barrier(jnp.sum(totals[:, 1:4] ** 2, axis=1))
    tensor_part = lax.optimization_barrier(jnp.sum(totals[:, 4:9] ** 2, axis=1))
    mixed = mix_layer[0] * scalar_part + mix_layer[1] * vector_part + mix_layer[2] * tensor_part
    active = jax.nn.silu(mixed).astype(jnp.bfloat16).reshape(-1, channels)
    return (hidden_features.astype(jnp.float32) + multiply(active, out_layer)).astype(jnp.bfloat16)

def reference(features, coords, counts, sources, wanted, pairs, lifting_weight, radial_weight, mix_weight, out_weight, force_weight):
    devices = N_GX * N_GY * N_GZ
    slot_count = TILES * TILE
    cell_edge = (slot_count / DENSITY) ** (1.0 / 3.0)
    shifts = jnp.asarray(offset_table()) * cell_edge
    whole_offsets = offset_table().astype(np.int32)
    flat_index = jnp.arange(devices).astype(jnp.int32)
    grid_x = flat_index // (N_GY * N_GZ)
    grid_y = flat_index // N_GZ % N_GY
    grid_z = flat_index % N_GZ
    neighbour_table = ((grid_x[:, None] + whole_offsets[None, :, 0]) % N_GX * (N_GY * N_GZ) + (grid_y[:, None] + whole_offsets[None, :, 1]) % N_GY * N_GZ + (grid_z[:, None] + whole_offsets[None, :, 2]) % N_GZ).astype(jnp.int32)
    slot_index = jnp.arange(slot_count).astype(jnp.int32)
    dead_place = FAR_AWAY + DEAD_SPACING * slot_index.astype(jnp.float32)
    start_place = jnp.where(slot_index[None, None, :] < counts.reshape(devices)[:, None, None], coords.reshape(devices, 3, slot_count), dead_place[None, None, :])
    anchor = sources.reshape(devices, slot_count).astype(jnp.int32)
    anchor_code = anchor // slot_count
    anchor_slot = anchor % slot_count
    anchor_device = neighbour_table[flat_index[:, None], anchor_code]
    hidden_features = features.reshape(devices, slot_count, C)[anchor_device, anchor_slot]
    places = start_place[anchor_device, :, anchor_slot] + shifts[anchor_code]
    places = jnp.transpose(places, (0, 2, 1))
    place_tiles = places.reshape(devices, 3, TILES, TILE)
    lists = wanted.reshape(devices, LAYERS, 27, GT).astype(jnp.int32)
    pair_lists = pairs.reshape(devices, 2, PAIRS).astype(jnp.int32)
    partial_value = jnp.zeros((devices, TILES + 27 * GT, 3, TILE), jnp.float32)
    for index_of_layer in range(LAYERS):
        projected_features = jnp.einsum('yri,iz->yrz', hidden_features.astype(jnp.float32), lifting_weight[index_of_layer].astype(jnp.float32), precision=lax.Precision.HIGHEST).astype(jnp.bfloat16)
        projected_tiles = projected_features.reshape(devices, TILES, TILE, C)
        with_force = index_of_layer == LAYERS - 1
        radial_layer = radial_weight[index_of_layer]

        def per_device(device_index):
            nearby = neighbour_table[device_index]
            chosen = lists[device_index, index_of_layer]
            ghost_rows = projected_tiles[nearby[:, None], chosen].reshape(27 * GT, TILE, C)
            ghost_places = (place_tiles[nearby[:, None], :, chosen] + shifts[:, None, :, None]).reshape(27 * GT, 3, TILE)
            local_places = jnp.transpose(place_tiles[device_index], (1, 0, 2))
            source_rows = jnp.concatenate([projected_tiles[device_index], ghost_rows], axis=0)
            source_places = jnp.concatenate([local_places, ghost_places], axis=0)
            pair_list = pair_lists[device_index]

            def one_pair(pair_index, carried):
                totals, partial_force = carried
                target = pair_list[0, pair_index]
                source = pair_list[1, pair_index]
                same_tile = (target == source).astype(jnp.float32)
                message, on_target, on_source = pair_terms(source_places[target], source_places[source], source_rows[target], source_rows[source], same_tile, radial_layer, force_weight, with_force)
                totals = totals.at[target].add(message)
                partial_force = partial_force.at[target].add(on_target).at[source].add(on_source)
                return (totals, partial_force)
            initial = (jnp.zeros((TILES, 9, TILE, C), jnp.float32), jnp.zeros((TILES + 27 * GT, 3, TILE), jnp.float32))
            totals, partial_force = lax.fori_loop(0, PAIRS, one_pair, initial)
            renewed = update(hidden_features[device_index], totals, mix_weight[index_of_layer], out_weight[index_of_layer])
            return (renewed, partial_force)
        hidden_features, partial_value = lax.map(per_device, flat_index)
    local_force = partial_value[:, :TILES]
    ghost_force = partial_value[:, TILES:].reshape(devices, 27, GT, 3 * TILE)
    facing = (26 - jnp.arange(27)).astype(jnp.int32)
    back_force = ghost_force[neighbour_table, facing[None, :]]
    back_tiles = lists[neighbour_table, LAYERS - 1, facing[None, :]]
    marks = (back_tiles[..., None] == jnp.arange(TILES)[None, None, None, :]).astype(jnp.float32)
    returned = jnp.einsum('dcgt,dcgx->dtx', marks, back_force, precision=lax.Precision.HIGHEST)
    total_force = local_force + returned.reshape(devices, TILES, 3, TILE)
    forces = jnp.transpose(total_force, (0, 2, 1, 3)).reshape(N_GX, N_GY, N_GZ, 3, TILES * TILE)
    updated = hidden_features.reshape(N_GX, N_GY, N_GZ, TILES * TILE, C)
    return (updated, forces)
```

```python
import math

import jax
import jax.numpy as jnp
import numpy as np
from jax import lax
from jax.experimental import pallas as pl
from jax.experimental.pallas import tpu as pltpu
from jax.sharding import PartitionSpec as P

NB = 8
TILE = 64
LAYERS = 2
PAIR_BLOCK = 2
LANES = 128
GROUPS = NB // 2
NEAR = 26
CAP = 32
AXES = ("gx", "gy", "gz")
MESH = pl.DeviceIdType.MESH

CUTOFF = 5.0
BASIS_WIDTH = 0.6
MESSAGE_SCALE = 0.2
SOFTENING = 0.25
FAR_AWAY = 1000.0
DEAD_SPACING = 100.0
DENSITY = 0.1
STEP = 4.2 / (NB - 1)


def padded(cells, sides, width):
    for axis, dim in sides:
        count = lax.axis_size(axis)
        head = lax.slice_in_dim(cells, 0, width, axis=dim)
        tail = lax.slice_in_dim(cells, cells.shape[dim] - width, cells.shape[dim], axis=dim)
        cells = jnp.concatenate(
            [
                lax.ppermute(tail, axis, [(i, (i + 1) % count) for i in range(count)]),
                cells,
                lax.ppermute(head, axis, [((i + 1) % count, i) for i in range(count)]),
            ],
            axis=dim,
        )
    return cells


def offset_table():
    return np.array(
        [
            [first_step, second_step, third_step]
            for first_step in (-1, 0, 1)
            for second_step in (-1, 0, 1)
            for third_step in (-1, 0, 1)
        ],
        dtype=np.float32,
    )


def harmonics(direction):
    along_x = direction[0]
    along_y = direction[1]
    along_z = direction[2]
    root_three = math.sqrt(3.0)
    root_five = math.sqrt(5.0)
    root_fifteen = math.sqrt(15.0)
    return jnp.stack(
        [
            jnp.ones_like(along_x),
            root_three * along_x,
            root_three * along_y,
            root_three * along_z,
            root_fifteen * along_x * along_y,
            root_fifteen * along_y * along_z,
            0.5 * root_five * (3.0 * along_z * along_z - 1.0),
            root_fifteen * along_x * along_z,
            0.5 * root_fifteen * (along_x * along_x - along_y * along_y),
        ]
    )


def multiply(left, right):
    return jnp.dot(left, right, preferred_element_type=jnp.float32)


def pair_terms(place_i, place_j, rows_i, rows_j, same_tile, radial_layer, force_weight, with_force):
    tile_size = place_i.shape[1]
    channels = rows_j.shape[1]
    wide_count = NB * tile_size
    place_wide = jnp.tile(place_j, (1, NB))
    separation = place_i[:, :, None] - place_wide[:, None, :]
    distance = jnp.sqrt(jnp.sum(separation * separation, axis=0) + SOFTENING)
    direction = separation / distance[None]
    centers = jnp.repeat(0.5 + jnp.arange(NB).astype(jnp.float32) * (4.2 / (NB - 1)), tile_size)
    ratio = jnp.minimum(distance / CUTOFF, 1.0)
    envelope = (1.0 - ratio * ratio) ** 2
    scaled = (distance - centers[None, :]) / BASIS_WIDTH
    keep_mask = 1.0 - same_tile * jnp.tile(jnp.eye(tile_size, dtype=jnp.float32), (1, NB))
    basis = jnp.exp(-scaled * scaled) * envelope * keep_mask
    angular = harmonics(direction)
    edges = (angular * basis[None]).astype(jnp.bfloat16)
    weighted = (radial_layer[:, :, None, :] * rows_j.astype(jnp.float32)[None, None]).astype(
        jnp.bfloat16
    )
    weighted = weighted.reshape(3, wide_count, channels)
    groups = ((0, 1), (1, 4), (4, 9))
    pieces = []
    for degree in range(3):
        start_row, stop_row = groups[degree]
        edge_block = edges[start_row:stop_row].reshape(
            (stop_row - start_row) * tile_size, wide_count
        )
        pieces.append(
            multiply(edge_block, weighted[degree]).reshape(
                stop_row - start_row, tile_size, channels
            )
        )
    message = jnp.concatenate(pieces, axis=0) * MESSAGE_SCALE
    if with_force:
        intersection = multiply(rows_i, rows_j.T) / math.sqrt(channels)
        basis_split = jnp.transpose(basis.reshape(tile_size, NB, tile_size), (1, 0, 2))
        profile = jnp.sum(force_weight[:, None, None] * basis_split, axis=0)
        narrow_direction = direction[:, :, :tile_size]
        pushes = (profile * intersection)[None] * narrow_direction
        return (message, 0.5 * jnp.sum(pushes, axis=2), -0.5 * jnp.sum(pushes, axis=1))
    nothing = jnp.zeros((3, tile_size), jnp.float32)
    return (message, nothing, nothing)


def update(hidden_features, totals, mix_layer, out_layer):
    channels = hidden_features.shape[1]
    scalar_part = totals[:, 0]
    vector_part = jnp.sum(totals[:, 1:4] ** 2, axis=1)
    tensor_part = jnp.sum(totals[:, 4:9] ** 2, axis=1)
    mixed = mix_layer[0] * scalar_part + mix_layer[1] * vector_part + mix_layer[2] * tensor_part
    active = jax.nn.silu(mixed).astype(jnp.bfloat16).reshape(-1, channels)
    return (hidden_features.astype(jnp.float32) + multiply(active, out_layer)).astype(jnp.bfloat16)


def opposite(grown, shape_out):
    return grown[0::2, 0::2, 0::2].reshape(shape_out)


def beside_all(placed):
    grown = padded(placed, (("gx", 0), ("gy", 1), ("gz", 2)), 1)
    return grown.reshape(27, 3, placed.shape[4])


def relay_rows(bundle):
    bundle = padded(bundle, (("gx", 0),), 1)[0::2]
    bundle = padded(bundle, (("gy", 1),), 1)[:, 0::2]
    return padded(bundle, (("gz", 2),), 1)[:, :, 0::2]


def relayed_force(bundle):
    bundle = padded(bundle, (("gx", 0),), 1)[0::2]
    bundle = padded(bundle, (("gy", 1),), 1)[:, 0::2]
    return padded(bundle, (("gz", 2),), 1)[:, :, 0::2]


def whole_path(
    features,
    coords,
    counts,
    sources,
    wanted,
    pairs,
    lifting_weight,
    radial_weight,
    mix_weight,
    out_weight,
    force_weight,
):
    slot_count = features.shape[3]
    channels = features.shape[4]
    tile_count = slot_count // TILE
    ghost_count = wanted.shape[5]
    pair_count = pairs.shape[4]
    cell_edge = (slot_count / DENSITY) ** (1.0 / 3.0)
    shifts = jnp.asarray(offset_table()) * cell_edge
    slot_index = jnp.arange(slot_count)
    dead_place = FAR_AWAY + DEAD_SPACING * slot_index.astype(jnp.float32)
    start_place = jnp.where(
        slot_index[None, :] < counts.reshape(()), coords.reshape(3, slot_count), dead_place[None, :]
    )
    anchor = sources.reshape(slot_count)
    gathered_rows = padded(features, (("gx", 0), ("gy", 1), ("gz", 2)), 1)
    hidden_features = jnp.take(gathered_rows.reshape(27 * slot_count, channels), anchor, axis=0)
    nearby_start = beside_all(start_place.reshape(1, 1, 1, 3, slot_count)) + shifts[:, :, None]
    places = jnp.take(
        jnp.transpose(nearby_start, (1, 0, 2)).reshape(3, 27 * slot_count), anchor, axis=1
    )
    nearby = beside_all(places.reshape(1, 1, 1, 3, slot_count)) + shifts[:, :, None]
    nearby_tiles = jnp.transpose(nearby.reshape(27, 3, tile_count, TILE), (0, 2, 1, 3)).reshape(
        27 * tile_count, 3, TILE
    )
    local_places = jnp.transpose(places.reshape(3, tile_count, TILE), (1, 0, 2))
    lists = wanted.reshape(LAYERS, 27, ghost_count)
    pair_list = pairs.reshape(2, pair_count)
    code_base = (jnp.arange(27) * tile_count)[:, None]
    cube_lists = jnp.transpose(lists, (1, 0, 2)).reshape(3, 3, 3, LAYERS, ghost_count)
    grown_lists = padded(cube_lists, (("gx", 0), ("gy", 1), ("gz", 2)), 1)
    requests = opposite(grown_lists, (27, LAYERS, ghost_count))
    partial_force = jnp.zeros((tile_count + 27 * ghost_count, 3, TILE), jnp.float32)
    for index_of_layer in range(LAYERS):
        projected_features = multiply(hidden_features, lifting_weight[index_of_layer]).astype(
            jnp.bfloat16
        )
        projected_tiles = projected_features.reshape(tile_count, TILE, channels)
        picked = (code_base + lists[index_of_layer]).reshape(-1)
        outgoing = jnp.take(projected_tiles, requests[:, index_of_layer].reshape(-1), axis=0)
        relayed = relay_rows(outgoing.reshape(3, 3, 3, ghost_count, TILE, channels))
        ghost_rows = relayed.reshape(27 * ghost_count, TILE, channels)
        ghost_places = jnp.take(nearby_tiles, picked, axis=0)
        source_rows = jnp.concatenate([projected_tiles, ghost_rows], axis=0)
        source_places = jnp.concatenate([local_places, ghost_places], axis=0)
        with_force = index_of_layer == LAYERS - 1
        radial_layer = radial_weight[index_of_layer]

        def pair_values(place_i, place_j, rows_i, rows_j, same_tile):
            return pair_terms(
                place_i, place_j, rows_i, rows_j, same_tile, radial_layer, force_weight, with_force
            )

        batched = jax.vmap(pair_values)

        def one_block(block_index, carried):
            totals, partial_value = carried
            targets = lax.dynamic_slice_in_dim(pair_list[0], block_index * PAIR_BLOCK, PAIR_BLOCK)
            anchors = lax.dynamic_slice_in_dim(pair_list[1], block_index * PAIR_BLOCK, PAIR_BLOCK)
            same_tile = (targets == anchors).astype(jnp.float32)
            message, on_target, on_source = batched(
                source_places[targets],
                source_places[anchors],
                source_rows[targets],
                source_rows[anchors],
                same_tile,
            )
            totals = totals.at[targets].add(message)
            partial_value = partial_value.at[targets].add(on_target).at[anchors].add(on_source)
            return (totals, partial_value)

        initial = (
            jnp.zeros((tile_count, 9, TILE, channels), jnp.float32),
            jnp.zeros((tile_count + 27 * ghost_count, 3, TILE), jnp.float32),
        )
        totals, partial_force = lax.fori_loop(0, pair_count // PAIR_BLOCK, one_block, initial)
        hidden_features = update(
            hidden_features, totals, mix_weight[index_of_layer], out_weight[index_of_layer]
        )
    own_force = partial_force[:tile_count]
    ghost_force = partial_force[tile_count:].reshape(27, ghost_count, 3 * TILE)
    tile_ids = jnp.arange(tile_count)
    arrived = relayed_force(ghost_force.reshape(3, 3, 3, ghost_count, 3 * TILE)).reshape(
        27, ghost_count, 3 * TILE
    )
    marks = (requests[:, LAYERS - 1][:, :, None] == tile_ids[None, None, :]).astype(jnp.float32)
    returned = jnp.einsum("cgt,cgx->tx", marks, arrived, precision=lax.Precision.HIGHEST)
    total_force = own_force + returned.reshape(tile_count, 3, TILE)
    forces = jnp.transpose(total_force, (1, 0, 2)).reshape(1, 1, 1, 3, slot_count)
    return (hidden_features.reshape(1, 1, 1, slot_count, channels), forces)


VMEM = pl.BlockSpec(memory_space=pltpu.VMEM)
SMEM = pl.BlockSpec(memory_space=pltpu.SMEM)


def code_of(n):
    return n + (1 if n >= 13 else 0)


def exchange_kernel(shared, axis, kinds, *refs):
    has_flag = axis is not None
    blocks = refs[:kinds]
    flag = refs[kinds] if has_flag else None
    landed = refs[kinds + has_flag : 2 * kinds + has_flag]
    rest = refs[2 * kinds + has_flag :]
    flags = rest[0] if has_flag else None
    rest = rest[has_flag:]
    send, receive = rest[0], rest[1]
    place = [lax.axis_index(name) for name in AXES]
    size = [lax.axis_size(name) for name in AXES]

    def beside(n):
        code = code_of(n)
        steps = (code // 9 - 1, code // 3 % 3 - 1, code % 3 - 1)
        return tuple(
            lax.rem(p + (step + s), s) if step else p for p, step, s in zip(place, steps, size)
        )

    def along(j):
        return tuple(
            lax.rem(p + j, s) if name == axis else p for p, name, s in zip(place, AXES, size)
        )

    count = size[AXES.index(axis)] if has_flag else 0
    barrier = pltpu.get_barrier_semaphore()
    for n in range(NEAR):
        pl.semaphore_signal(barrier, inc=1, device_id=beside(n), device_id_type=MESH)
    for j in range(1, count):
        pl.semaphore_signal(barrier, inc=1, device_id=along(j), device_id_type=MESH)
    pl.semaphore_wait(barrier, NEAR + max(count - 1, 0))

    copies = []
    for n in range(NEAR):
        for kind in range(kinds):
            copies.append(
                pltpu.make_async_remote_copy(
                    src_ref=blocks[kind].at[0 if shared else n],
                    dst_ref=landed[kind].at[NEAR - 1 - n],
                    send_sem=send.at[kind, n],
                    recv_sem=receive.at[kind, NEAR - 1 - n],
                    device_id=beside(n),
                    device_id_type=MESH,
                )
            )
    for j in range(1, count):
        copies.append(
            pltpu.make_async_remote_copy(
                src_ref=flag,
                dst_ref=flags.at[j],
                send_sem=rest[2].at[j],
                recv_sem=rest[3].at[j],
                device_id=along(j),
                device_id_type=MESH,
            )
        )
    for copy in copies:
        copy.start()
    for copy in copies:
        copy.wait()


def exchange(identity, blocks, shared=False, flag=None, axis=None):
    kinds = len(blocks)
    shape = jax.ShapeDtypeStruct
    outs = [shape((NEAR,) + b.shape[1:], b.dtype) for b in blocks]
    scratch = [pltpu.SemaphoreType.DMA((kinds, NEAR)), pltpu.SemaphoreType.DMA((kinds, NEAR))]
    operands = list(blocks)
    if flag is not None:
        around = lax.axis_size(axis)
        outs.append(shape((around,) + flag.shape, flag.dtype))
        scratch += [pltpu.SemaphoreType.DMA((around,)), pltpu.SemaphoreType.DMA((around,))]
        operands.append(flag)

    def kernel(*refs):
        exchange_kernel(shared, axis, kinds, *refs)

    return pl.pallas_call(
        kernel,
        name=f"exchange_{identity}",
        out_shape=outs,
        in_specs=[VMEM] * len(operands),
        out_specs=[VMEM] * len(outs),
        scratch_shapes=scratch,
        compiler_params=pltpu.CompilerParams(collective_id=identity, has_side_effects=True),
    )(*operands)


def raised(own, flags):
    found = own[...]
    for j in range(1, flags.shape[0]):
        found = jnp.maximum(found, flags[j])
    return found


def three_parts(values):
    high = values.astype(jnp.bfloat16).astype(jnp.float32)
    middle = (values - high).astype(jnp.bfloat16).astype(jnp.float32)
    low = values - high - middle
    return jnp.concatenate([high, middle, low], axis=0).astype(jnp.bfloat16)


def joined(parts):
    return parts[0:8] + parts[8:16] + parts[16:24]


def across(left, right):
    return lax.dot_general(left, right, (((1,), (1,)), ((), ())), preferred_element_type=jnp.float32)


def iota(shape, dim):
    return lax.broadcasted_iota(jnp.int32, shape, dim)


def picked_start(coords, count):
    slots = coords.shape[1]
    slot = iota((3, slots), 1)
    start = jnp.where(slot < count, coords[...], FAR_AWAY + DEAD_SPACING * slot.astype(jnp.float32))
    return jnp.concatenate([start, jnp.zeros((5, slots), jnp.float32)], axis=0)


def send_kernel(counts, lists, features, coords, rows_out, spots_out, flag_out, table):
    slots = features.shape[0]
    table[...] = jnp.zeros_like(table)
    for n in range(NEAR):
        for part in range(slots // LANES):
            table[n : n + 1, part * LANES : (part + 1) * LANES] = lists[n, part : part + 1, :]
    held = table[...]
    row = iota(held.shape, 0)
    code = row + jnp.where(row >= 13, 1, 0)
    mine = jnp.logical_and(lax.shift_right_logical(held, 9) == 26 - code, row < NEAR)
    slot = jnp.bitwise_and(held, 511).astype(jnp.float32)
    before = (iota((slots, slots), 0) < iota((slots, slots), 1)).astype(jnp.float32)
    chosen = jnp.where(mine, 1.0, 0.0)
    rank = jnp.dot(
        chosen.astype(jnp.bfloat16), before.astype(jnp.bfloat16), preferred_element_type=jnp.float32
    )
    rank = jnp.where(mine, rank, -1.0)
    many = jnp.max(jnp.sum(chosen, axis=1, keepdims=True))
    flag_out[...] = jnp.full((8, LANES), jnp.where(many > CAP, 1, 0), jnp.int32)
    parts = three_parts(picked_start(coords, counts[0]))
    order = iota((CAP, slots), 0).astype(jnp.float32)
    lane = iota((CAP, slots), 1).astype(jnp.float32)
    spots_out[...] = jnp.zeros_like(spots_out)
    for n in range(NEAR):
        hit = rank[n : n + 1, :] == order
        place = jnp.sum(jnp.where(hit, slot[n : n + 1, :], 0.0), axis=1, keepdims=True)
        select = (place == lane).astype(jnp.float32).astype(jnp.bfloat16)
        rows_out[n] = jnp.dot(select, features[...], preferred_element_type=jnp.float32).astype(
            jnp.bfloat16
        )
        spots_out[n, :, 0:CAP] = joined(across(parts, select))


def take_kernel(
    edge,
    counts,
    list_block,
    lists,
    features,
    coords,
    rows_in,
    spots_in,
    flag_in,
    flags,
    lift,
    hidden_out,
    rows_out,
    spots_out,
    asked_rows,
    asked_spots,
    wants_out,
    flag_out,
    gathered,
    beside,
    select,
    ready,
):
    slots, channels = features.shape
    tiles = slots // TILE
    own_base = gathered.shape[0] - slots
    bring = pltpu.make_async_copy(lists.at[:, 4, :], wants_out, ready)
    bring.start()
    flag_out[...] = raised(flag_in, flags)
    row_parts = [list_block[0, part : part + 1, :] for part in range(slots // LANES)]
    row_all = jnp.concatenate(row_parts, axis=1)
    code_row = lax.shift_right_logical(row_all, 9)
    code_row_f = code_row.astype(jnp.float32)
    for first in range(slots // LANES):
        turned = jnp.transpose(
            jnp.broadcast_to(row_parts[first].astype(jnp.float32), (LANES, LANES))
        ).astype(jnp.int32)
        code = lax.shift_right_logical(turned, 9)
        slot = jnp.bitwise_and(turned, 511)
        code_f = code.astype(jnp.float32)
        total = jnp.zeros((LANES, LANES), jnp.float32)
        level = iota((LANES, LANES), 0)
        lane = iota((LANES, LANES), 1)
        for second in range(first + 1):
            same = code_f == code_row_f[:, second * LANES : (second + 1) * LANES]
            if second == first:
                same = jnp.logical_and(same, lane < level)
            total = total + jnp.where(same, 1.0, 0.0)
        rank = jnp.sum(total, axis=1, keepdims=True).astype(jnp.int32)
        neighbour = code - jnp.where(code >= 13, 1, 0)
        index = jnp.where(code == 13, own_base + slot, neighbour * CAP + rank)
        for block in range(gathered.shape[0] // LANES):
            hit = index == lane + block * LANES
            select[first * LANES : (first + 1) * LANES, block * LANES : (block + 1) * LANES] = (
                jnp.where(hit, 1.0, 0.0).astype(jnp.bfloat16)
            )
    taken = NEAR * CAP
    gathered[0:taken, :] = rows_in[...].reshape(taken, channels)
    gathered[taken:own_base, :] = jnp.zeros((own_base - taken, channels), jnp.bfloat16)
    gathered[own_base:, :] = features[...]
    beside[:, 0:own_base] = jnp.zeros((8, own_base), jnp.float32)
    for n in range(NEAR):
        beside[:, n * CAP : (n + 1) * CAP] = spots_in[n, :, 0:CAP]
    beside[:, own_base:] = picked_start(coords, counts[0])
    hidden = jnp.dot(select[...], gathered[...], preferred_element_type=jnp.float32).astype(jnp.bfloat16)
    hidden_out[...] = hidden.reshape(hidden_out.shape)
    projected = jnp.dot(hidden, lift[...], preferred_element_type=jnp.float32).astype(jnp.bfloat16)
    rows_out[...] = projected.reshape(rows_out.shape)
    placed = joined(across(three_parts(beside[...]), select[...]))
    high = jnp.where(code_row >= 9, 1, 0) + jnp.where(code_row >= 18, 1, 0)
    rest = code_row - 9 * high
    middle = jnp.where(rest >= 3, 1, 0) + jnp.where(rest >= 6, 1, 0)
    low = rest - 3 * middle
    line = iota((8, slots), 0)
    shift = jnp.where(line == 0, high - 1, jnp.where(line == 1, middle - 1, low - 1))
    placed = placed + shift.astype(jnp.float32) * edge
    half = iota((8, LANES), 1) < TILE
    for t in range(tiles):
        part = placed[:, t // 2 * LANES : (t // 2 + 1) * LANES]
        swapped = pltpu.roll(part, TILE, 1)
        spots_out[t] = jnp.where(half, part, swapped) if t % 2 == 0 else jnp.where(half, swapped, part)
    bring.wait()
    for n in range(NEAR):
        reader = 26 - code_of(n)
        asked_rows[n] = rows_out[wants_out[n, reader]]
        near = spots_out[wants_out[n, reader]]
        later = pltpu.roll(spots_out[wants_out[n, 32 + reader]], 3, 0)
        asked_spots[n] = jnp.where(iota((8, LANES), 0) < 3, near, later)


def layer_kernel(with_force, edge, pairs, force_weight, wants, own_rows, near_rows, own_spots, near_spots, *refs):
    if with_force:
        (hidden, radial, mix, out_weight, flag_in, flags) = refs[:6]
        (renewed, own_force, near_force, flag_out) = refs[6:10]
        (rows, spots, totals, wide, edges, weighted, on_target, on_source) = refs[10:]
    else:
        (hidden, radial, mix, out_weight, flag_in, flags, lift) = refs[:7]
        (renewed, projected, asked, flag_out) = refs[7:11]
        (rows, spots, totals, wide, edges, weighted) = refs[11:]
    tiles = hidden.shape[0]
    channels = rows.shape[2]
    flag_out[...] = raised(flag_in, flags)
    half = iota((TILE, LANES), 1) // TILE
    within = iota((TILE, LANES), 1) % TILE
    eye = (within == iota((TILE, LANES), 0)).astype(jnp.float32)
    upper = half.astype(jnp.float32)
    totals[...] = jnp.zeros_like(totals)
    rows[0:tiles] = own_rows[...]
    spots[0:tiles] = own_spots[...]
    rows[tiles + 13] = jnp.zeros(rows.shape[1:], rows.dtype)
    spots[tiles + 13] = jnp.zeros(spots.shape[1:], spots.dtype)
    for n in range(NEAR):
        code = code_of(n)
        rows[tiles + code] = near_rows[n]
        steps = (code // 9 - 1, code // 3 % 3 - 1, code % 3 - 1)
        for axis in range(3):
            line = axis + (3 if with_force else 0)
            spots[tiles + code, axis : axis + 1, :] = near_spots[n, line : line + 1, :] + steps[axis] * edge
    if with_force:
        on_target[...] = jnp.zeros_like(on_target)
        on_source[...] = jnp.zeros_like(on_source)
    for t in range(tiles):
        turned = jnp.transpose(jnp.broadcast_to(spots[t][None], (16, 8, LANES)).reshape(LANES, LANES))
        for axis in range(3):
            wide[t, axis] = jnp.broadcast_to(turned[:TILE, axis : axis + 1], (TILE, LANES))

    def one_pair(pair, slot):
        target = pairs[0, pair]
        source = pairs[1, pair]
        same = jnp.where(target == source, 1.0, 0.0).astype(jnp.float32)
        spot = spots[source]
        gap = [wide[target, axis] - spot[axis : axis + 1, :] for axis in range(3)]
        square = gap[0] * gap[0] + gap[1] * gap[1] + gap[2] * gap[2] + SOFTENING
        inverse = lax.rsqrt(square)
        distance = square * inverse
        ramp = 1.0 - jnp.minimum(square * (1.0 / (CUTOFF * CUTOFF)), 1.0)
        envelope = ramp * ramp * (1.0 - same * eye)
        unit = [g * inverse for g in gap]
        scaled = (distance - (0.5 + STEP * upper)) * (1.0 / BASIS_WIDTH)
        root_three = math.sqrt(3.0)
        root_five = math.sqrt(5.0)
        root_fifteen = math.sqrt(15.0)
        fifteen = [root_fifteen * u for u in unit]
        angular = [
            None,
            root_three * unit[0],
            root_three * unit[1],
            root_three * unit[2],
            fifteen[0] * unit[1],
            fifteen[1] * unit[2],
            (1.5 * root_five) * unit[2] * unit[2] - 0.5 * root_five,
            fifteen[0] * unit[2],
            0.5 * (fifteen[0] * unit[0] - fifteen[1] * unit[1]),
        ]
        profile = None
        for q in range(GROUPS):
            moved = scaled - (2.0 * q * STEP / BASIS_WIDTH)
            basis = jnp.exp(-(moved * moved)) * envelope
            if with_force:
                weight = jnp.where(half == 0, force_weight[2 * q], force_weight[2 * q + 1])
                profile = weight * basis if profile is None else profile + weight * basis
            columns = slice(q * LANES, (q + 1) * LANES)
            edges[slot, 0:TILE, columns] = basis.astype(jnp.bfloat16)
            for m in range(1, 9):
                edges[slot, m * TILE : (m + 1) * TILE, columns] = (angular[m] * basis).astype(jnp.bfloat16)
        near = rows[source]
        full = near.astype(jnp.float32)
        for k in range(3 * NB):
            weighted[slot, k // NB, (k % NB) * TILE : (k % NB + 1) * TILE, :] = (
                full * radial[k : k + 1, :]
            ).astype(jnp.bfloat16)
        for order, (low, high) in enumerate(((0, 1), (1, 4), (4, 9))):
            message = multiply(edges[slot, low * TILE : high * TILE, :], weighted[slot, order])
            totals[target, low * TILE : high * TILE, :] += message
        if with_force:
            twice = jnp.concatenate([near, near], axis=0)
            strength = profile * across(rows[target], twice)
            for axis in range(3):
                push = strength * unit[axis]
                on_target[target, axis] += push
                on_source[source, axis] += jnp.sum(push.reshape(TILE // 8, 8, LANES), axis=0)

    count = pairs.shape[1]

    def two_pairs(step, carried):
        one_pair(2 * step, 0)
        one_pair(2 * step + 1, 1)
        return carried

    lax.fori_loop(0, count // 2, two_pairs, 0)
    for left in range(count // 2 * 2, count):
        one_pair(left, 0)

    def one_tile(t, carried):
        def part(m):
            return totals[t, m * TILE : (m + 1) * TILE, :] * MESSAGE_SCALE

        vector = part(1) ** 2 + part(2) ** 2 + part(3) ** 2
        tensor = part(4) ** 2 + part(5) ** 2 + part(6) ** 2 + part(7) ** 2 + part(8) ** 2
        mixed = mix[0:1, :] * part(0) + mix[1:2, :] * vector + mix[2:3, :] * tensor
        active = (mixed / (1.0 + jnp.exp(-mixed))).astype(jnp.bfloat16)
        fresh = (hidden[t].astype(jnp.float32) + multiply(active, out_weight[...])).astype(jnp.bfloat16)
        renewed[t] = fresh
        if not with_force:
            projected[t] = multiply(fresh, lift[...]).astype(jnp.bfloat16)
        return carried

    lax.fori_loop(0, tiles, one_tile, 0)
    if not with_force:
        for n in range(NEAR):
            asked[n] = projected[wants[n, 32 + 26 - code_of(n)]]
    else:
        factor = 0.5 / math.sqrt(channels)
        lane = iota((TILE, LANES), 1)
        line = iota((8, LANES), 0)

        def folded(b):
            sums = jnp.zeros((8, LANES), jnp.float32)
            for axis in range(3):
                summed = jnp.sum(on_source[b, axis], axis=0, keepdims=True)
                sums = jnp.where(line == axis, jnp.broadcast_to(summed, (8, LANES)), sums)
            return (sums + pltpu.roll(sums, TILE, 1)) * factor

        for t in range(tiles):
            columns = jnp.zeros((TILE, LANES), jnp.float32)
            for axis in range(3):
                summed = jnp.sum(on_target[t, axis], axis=1, keepdims=True)
                columns = jnp.where(lane == axis, summed, columns)
            turned = jnp.transpose(jnp.concatenate([columns, columns], axis=0))[0:8, :]
            own_force[t] = turned * factor - folded(t)
        for n in range(NEAR):
            near_force[n] = -folded(tiles + code_of(n))


def force_kernel(wants, own_force, arrived, forces, total):
    total[...] = own_force[...]
    for n in range(NEAR):
        tile = wants[n, 32 + 26 - code_of(n)]
        total[tile] += arrived[n]
    half = iota((8, LANES), 1) < TILE
    for block in range(total.shape[0] // 2):
        both = jnp.where(half, total[2 * block], total[2 * block + 1])
        forces[:, block * LANES : (block + 1) * LANES] = both[0:3, :]


def call(kernel, name, out_shape, in_specs, out_specs, scratch, operands):
    return pl.pallas_call(
        kernel,
        name=name,
        out_shape=out_shape,
        in_specs=in_specs,
        out_specs=out_specs,
        scratch_shapes=scratch,
        compiler_params=pltpu.CompilerParams(vmem_limit_bytes=40 * 1024 * 1024),
    )(*operands)


def body(
    features,
    coords,
    counts,
    sources,
    wanted,
    pairs,
    lifting_weight,
    radial_weight,
    mix_weight,
    out_weight,
    force_weight,
):
    slots, channels = features.shape[3], features.shape[4]
    tiles = slots // TILE
    edge = float((slots / DENSITY) ** (1.0 / 3.0))
    shape = jax.ShapeDtypeStruct
    flat_features = features.reshape(slots, channels)
    flat_coords = coords.reshape(3, slots)
    flat_counts = counts.reshape(1)
    pair_list = pairs.reshape(2, pairs.shape[4])
    wants = jnp.pad(wanted.reshape(LAYERS, 27), ((0, 0), (0, 5))).reshape(1, LAYERS * 32)
    list_block = jnp.concatenate(
        [
            sources.reshape(slots // LANES, LANES),
            jnp.pad(wants, ((0, 3), (0, LANES - LAYERS * 32))),
        ],
        axis=0,
    )[None]
    (lists,) = exchange(1, [list_block], shared=True)
    tile_shape = shape((tiles, TILE, channels), jnp.bfloat16)
    spot_shape = shape((tiles, 8, LANES), jnp.float32)
    near_tiles = shape((NEAR, TILE, channels), jnp.bfloat16)
    near_spots = shape((NEAR, 8, LANES), jnp.float32)
    flag_shape = shape((8, LANES), jnp.int32)
    moved_rows, moved_spots, flag = call(
        send_kernel,
        "send_rows",
        [shape((NEAR, CAP, channels), jnp.bfloat16), near_spots, flag_shape],
        [SMEM, VMEM, VMEM, VMEM],
        [VMEM] * 3,
        [pltpu.VMEM((32, slots), jnp.int32)],
        (flat_counts, lists, flat_features, flat_coords),
    )
    rows_in, spots_in, flags = exchange(2, [moved_rows, moved_spots], flag=flag, axis="gx")
    held = -(-NEAR * CAP // LANES) * LANES + slots

    def take(*refs):
        take_kernel(edge, *refs)

    hidden, own_rows, own_spots, asked_rows, asked_spots, wants_list, flag = call(
        take,
        "take_rows",
        [tile_shape, tile_shape, spot_shape, near_tiles, near_spots, shape((NEAR, LANES), jnp.int32), flag_shape],
        [SMEM] + [VMEM] * 9,
        [VMEM] * 5 + [SMEM, VMEM],
        [
            pltpu.VMEM((held, channels), jnp.bfloat16),
            pltpu.VMEM((8, held), jnp.float32),
            pltpu.VMEM((slots, held), jnp.bfloat16),
            pltpu.SemaphoreType.DMA,
        ],
        (
            flat_counts,
            list_block,
            lists,
            flat_features,
            flat_coords,
            rows_in,
            spots_in,
            flag,
            flags,
            lifting_weight[0],
        ),
    )
    near_rows, near_places, flags = exchange(3, [asked_rows, asked_spots], flag=flag, axis="gy")
    scratch = [
        pltpu.VMEM((tiles + 27, TILE, channels), jnp.bfloat16),
        pltpu.VMEM((tiles + 27, 8, LANES), jnp.float32),
        pltpu.VMEM((tiles, 9 * TILE, channels), jnp.float32),
        pltpu.VMEM((tiles, 3, TILE, LANES), jnp.float32),
        pltpu.VMEM((2, 9 * TILE, NB * TILE), jnp.bfloat16),
        pltpu.VMEM((2, 3, NB * TILE, channels), jnp.bfloat16),
    ]

    def first(*refs):
        layer_kernel(False, edge, *refs)

    def last(*refs):
        layer_kernel(True, edge, *refs)

    hidden, own_rows, asked_rows, flag = call(
        first,
        "layer_first",
        [tile_shape, tile_shape, near_tiles, flag_shape],
        [SMEM] * 3 + [VMEM] * 11,
        [VMEM] * 4,
        scratch,
        (
            pair_list,
            force_weight,
            wants_list,
            own_rows,
            near_rows,
            own_spots,
            near_places,
            hidden,
            radial_weight[0].reshape(3 * NB, channels),
            mix_weight[0],
            out_weight[0],
            flag,
            flags,
            lifting_weight[1],
        ),
    )
    near_rows, flags = exchange(4, [asked_rows], flag=flag, axis="gz")
    updated, own_force, near_force, flag = call(
        last,
        "layer_last",
        [tile_shape, spot_shape, near_spots, flag_shape],
        [SMEM] * 3 + [VMEM] * 10,
        [VMEM] * 4,
        scratch
        + [
            pltpu.VMEM((tiles, 3, TILE, LANES), jnp.float32),
            pltpu.VMEM((tiles + 27, 3, 8, LANES), jnp.float32),
        ],
        (
            pair_list,
            force_weight,
            wants_list,
            own_rows,
            near_rows,
            own_spots,
            near_places,
            hidden,
            radial_weight[1].reshape(3 * NB, channels),
            mix_weight[1],
            out_weight[1],
            flag,
            flags,
        ),
    )
    (arrived,) = exchange(5, [near_force])
    (forces,) = call(
        force_kernel,
        "add_forces",
        [shape((3, slots), jnp.float32)],
        [SMEM, VMEM, VMEM],
        [VMEM],
        [pltpu.VMEM((tiles, 8, LANES), jnp.float32)],
        (wants_list, own_force, arrived),
    )
    updated = updated.reshape(features.shape)
    forces = forces.reshape(coords.shape)
    return lax.cond(
        flag[0, 0] > 0,
        lambda: whole_path(
            features,
            coords,
            counts,
            sources,
            wanted,
            pairs,
            lifting_weight,
            radial_weight,
            mix_weight,
            out_weight,
            force_weight,
        ),
        lambda: (updated, forces),
    )


def solution(mesh):
    placed = (
        P("gx", "gy", "gz", None, None),
        P("gx", "gy", "gz", None, None),
        P("gx", "gy", "gz"),
        P("gx", "gy", "gz", None),
        P("gx", "gy", "gz", None, None, None),
        P("gx", "gy", "gz", None, None),
        P(),
        P(),
        P(),
        P(),
        P(),
    )
    return jax.shard_map(
        body,
        mesh=mesh,
        in_specs=placed,
        out_specs=(P("gx", "gy", "gz", None, None), P("gx", "gy", "gz", None, None)),
        check_vma=False,
    )
```

```python
import math

import jax
import jax.numpy as jnp
import numpy as np
from jax import lax
from jax.experimental import pallas as pl
from jax.experimental.pallas import tpu as pltpu
from jax.sharding import PartitionSpec as P

NB = 8
TILE = 64
LAYERS = 2
PAIR_BLOCK = 2
LANES = 128
GROUPS = NB // 2
NEAR = 26
CAP = 32
AXES = ("gx", "gy", "gz")
MESH = pl.DeviceIdType.MESH

CUTOFF = 5.0
BASIS_WIDTH = 0.6
MESSAGE_SCALE = 0.2
SOFTENING = 0.25
FAR_AWAY = 1000.0
DEAD_SPACING = 100.0
DENSITY = 0.1
STEP = 4.2 / (NB - 1)


def padded(cells, sides, width):
    for axis, dim in sides:
        count = lax.axis_size(axis)
        head = lax.slice_in_dim(cells, 0, width, axis=dim)
        tail = lax.slice_in_dim(cells, cells.shape[dim] - width, cells.shape[dim], axis=dim)
        cells = jnp.concatenate(
            [
                lax.ppermute(tail, axis, [(i, (i + 1) % count) for i in range(count)]),
                cells,
                lax.ppermute(head, axis, [((i + 1) % count, i) for i in range(count)]),
            ],
            axis=dim,
        )
    return cells


def offset_table():
    return np.array(
        [
            [first_step, second_step, third_step]
            for first_step in (-1, 0, 1)
            for second_step in (-1, 0, 1)
            for third_step in (-1, 0, 1)
        ],
        dtype=np.float32,
    )


def harmonics(direction):
    along_x = direction[0]
    along_y = direction[1]
    along_z = direction[2]
    root_three = math.sqrt(3.0)
    root_five = math.sqrt(5.0)
    root_fifteen = math.sqrt(15.0)
    return jnp.stack(
        [
            jnp.ones_like(along_x),
            root_three * along_x,
            root_three * along_y,
            root_three * along_z,
            root_fifteen * along_x * along_y,
            root_fifteen * along_y * along_z,
            0.5 * root_five * (3.0 * along_z * along_z - 1.0),
            root_fifteen * along_x * along_z,
            0.5 * root_fifteen * (along_x * along_x - along_y * along_y),
        ]
    )


def multiply(left, right):
    return jnp.dot(left, right, preferred_element_type=jnp.float32)


def pair_terms(place_i, place_j, rows_i, rows_j, same_tile, radial_layer, force_weight, with_force):
    tile_size = place_i.shape[1]
    channels = rows_j.shape[1]
    wide_count = NB * tile_size
    place_wide = jnp.tile(place_j, (1, NB))
    separation = place_i[:, :, None] - place_wide[:, None, :]
    distance = jnp.sqrt(jnp.sum(separation * separation, axis=0) + SOFTENING)
    direction = separation / distance[None]
    centers = jnp.repeat(0.5 + jnp.arange(NB).astype(jnp.float32) * (4.2 / (NB - 1)), tile_size)
    ratio = jnp.minimum(distance / CUTOFF, 1.0)
    envelope = (1.0 - ratio * ratio) ** 2
    scaled = (distance - centers[None, :]) / BASIS_WIDTH
    keep_mask = 1.0 - same_tile * jnp.tile(jnp.eye(tile_size, dtype=jnp.float32), (1, NB))
    basis = jnp.exp(-scaled * scaled) * envelope * keep_mask
    angular = harmonics(direction)
    edges = (angular * basis[None]).astype(jnp.bfloat16)
    weighted = (radial_layer[:, :, None, :] * rows_j.astype(jnp.float32)[None, None]).astype(
        jnp.bfloat16
    )
    weighted = weighted.reshape(3, wide_count, channels)
    groups = ((0, 1), (1, 4), (4, 9))
    pieces = []
    for degree in range(3):
        start_row, stop_row = groups[degree]
        edge_block = edges[start_row:stop_row].reshape(
            (stop_row - start_row) * tile_size, wide_count
        )
        pieces.append(
            multiply(edge_block, weighted[degree]).reshape(
                stop_row - start_row, tile_size, channels
            )
        )
    message = jnp.concatenate(pieces, axis=0) * MESSAGE_SCALE
    if with_force:
        intersection = multiply(rows_i, rows_j.T) / math.sqrt(channels)
        basis_split = jnp.transpose(basis.reshape(tile_size, NB, tile_size), (1, 0, 2))
        profile = jnp.sum(force_weight[:, None, None] * basis_split, axis=0)
        narrow_direction = direction[:, :, :tile_size]
        pushes = (profile * intersection)[None] * narrow_direction
        return (message, 0.5 * jnp.sum(pushes, axis=2), -0.5 * jnp.sum(pushes, axis=1))
    nothing = jnp.zeros((3, tile_size), jnp.float32)
    return (message, nothing, nothing)


def update(hidden_features, totals, mix_layer, out_layer):
    channels = hidden_features.shape[1]
    scalar_part = totals[:, 0]
    vector_part = jnp.sum(totals[:, 1:4] ** 2, axis=1)
    tensor_part = jnp.sum(totals[:, 4:9] ** 2, axis=1)
    mixed = mix_layer[0] * scalar_part + mix_layer[1] * vector_part + mix_layer[2] * tensor_part
    active = jax.nn.silu(mixed).astype(jnp.bfloat16).reshape(-1, channels)
    return (hidden_features.astype(jnp.float32) + multiply(active, out_layer)).astype(jnp.bfloat16)


def opposite(grown, shape_out):
    return grown[0::2, 0::2, 0::2].reshape(shape_out)


def beside_all(placed):
    grown = padded(placed, (("gx", 0), ("gy", 1), ("gz", 2)), 1)
    return grown.reshape(27, 3, placed.shape[4])


def relay_rows(bundle):
    bundle = padded(bundle, (("gx", 0),), 1)[0::2]
    bundle = padded(bundle, (("gy", 1),), 1)[:, 0::2]
    return padded(bundle, (("gz", 2),), 1)[:, :, 0::2]


def relayed_force(bundle):
    bundle = padded(bundle, (("gx", 0),), 1)[0::2]
    bundle = padded(bundle, (("gy", 1),), 1)[:, 0::2]
    return padded(bundle, (("gz", 2),), 1)[:, :, 0::2]


def whole_path(
    features,
    coords,
    counts,
    sources,
    wanted,
    pairs,
    lifting_weight,
    radial_weight,
    mix_weight,
    out_weight,
    force_weight,
):
    slot_count = features.shape[3]
    channels = features.shape[4]
    tile_count = slot_count // TILE
    ghost_count = wanted.shape[5]
    pair_count = pairs.shape[4]
    cell_edge = (slot_count / DENSITY) ** (1.0 / 3.0)
    shifts = jnp.asarray(offset_table()) * cell_edge
    slot_index = jnp.arange(slot_count)
    dead_place = FAR_AWAY + DEAD_SPACING * slot_index.astype(jnp.float32)
    start_place = jnp.where(
        slot_index[None, :] < counts.reshape(()), coords.reshape(3, slot_count), dead_place[None, :]
    )
    anchor = sources.reshape(slot_count)
    gathered_rows = padded(features, (("gx", 0), ("gy", 1), ("gz", 2)), 1)
    hidden_features = jnp.take(gathered_rows.reshape(27 * slot_count, channels), anchor, axis=0)
    nearby_start = beside_all(start_place.reshape(1, 1, 1, 3, slot_count)) + shifts[:, :, None]
    places = jnp.take(
        jnp.transpose(nearby_start, (1, 0, 2)).reshape(3, 27 * slot_count), anchor, axis=1
    )
    nearby = beside_all(places.reshape(1, 1, 1, 3, slot_count)) + shifts[:, :, None]
    nearby_tiles = jnp.transpose(nearby.reshape(27, 3, tile_count, TILE), (0, 2, 1, 3)).reshape(
        27 * tile_count, 3, TILE
    )
    local_places = jnp.transpose(places.reshape(3, tile_count, TILE), (1, 0, 2))
    lists = wanted.reshape(LAYERS, 27, ghost_count)
    pair_list = pairs.reshape(2, pair_count)
    code_base = (jnp.arange(27) * tile_count)[:, None]
    cube_lists = jnp.transpose(lists, (1, 0, 2)).reshape(3, 3, 3, LAYERS, ghost_count)
    grown_lists = padded(cube_lists, (("gx", 0), ("gy", 1), ("gz", 2)), 1)
    requests = opposite(grown_lists, (27, LAYERS, ghost_count))
    partial_force = jnp.zeros((tile_count + 27 * ghost_count, 3, TILE), jnp.float32)
    for index_of_layer in range(LAYERS):
        projected_features = multiply(hidden_features, lifting_weight[index_of_layer]).astype(
            jnp.bfloat16
        )
        projected_tiles = projected_features.reshape(tile_count, TILE, channels)
        picked = (code_base + lists[index_of_layer]).reshape(-1)
        outgoing = jnp.take(projected_tiles, requests[:, index_of_layer].reshape(-1), axis=0)
        relayed = relay_rows(outgoing.reshape(3, 3, 3, ghost_count, TILE, channels))
        ghost_rows = relayed.reshape(27 * ghost_count, TILE, channels)
        ghost_places = jnp.take(nearby_tiles, picked, axis=0)
        source_rows = jnp.concatenate([projected_tiles, ghost_rows], axis=0)
        source_places = jnp.concatenate([local_places, ghost_places], axis=0)
        with_force = index_of_layer == LAYERS - 1
        radial_layer = radial_weight[index_of_layer]

        def pair_values(place_i, place_j, rows_i, rows_j, same_tile):
            return pair_terms(
                place_i, place_j, rows_i, rows_j, same_tile, radial_layer, force_weight, with_force
            )

        batched = jax.vmap(pair_values)

        def one_block(block_index, carried):
            totals, partial_value = carried
            targets = lax.dynamic_slice_in_dim(pair_list[0], block_index * PAIR_BLOCK, PAIR_BLOCK)
            anchors = lax.dynamic_slice_in_dim(pair_list[1], block_index * PAIR_BLOCK, PAIR_BLOCK)
            same_tile = (targets == anchors).astype(jnp.float32)
            message, on_target, on_source = batched(
                source_places[targets],
                source_places[anchors],
                source_rows[targets],
                source_rows[anchors],
                same_tile,
            )
            totals = totals.at[targets].add(message)
            partial_value = partial_value.at[targets].add(on_target).at[anchors].add(on_source)
            return (totals, partial_value)

        initial = (
            jnp.zeros((tile_count, 9, TILE, channels), jnp.float32),
            jnp.zeros((tile_count + 27 * ghost_count, 3, TILE), jnp.float32),
        )
        totals, partial_force = lax.fori_loop(0, pair_count // PAIR_BLOCK, one_block, initial)
        hidden_features = update(
            hidden_features, totals, mix_weight[index_of_layer], out_weight[index_of_layer]
        )
    own_force = partial_force[:tile_count]
    ghost_force = partial_force[tile_count:].reshape(27, ghost_count, 3 * TILE)
    tile_ids = jnp.arange(tile_count)
    arrived = relayed_force(ghost_force.reshape(3, 3, 3, ghost_count, 3 * TILE)).reshape(
        27, ghost_count, 3 * TILE
    )
    marks = (requests[:, LAYERS - 1][:, :, None] == tile_ids[None, None, :]).astype(jnp.float32)
    returned = jnp.einsum("cgt,cgx->tx", marks, arrived, precision=lax.Precision.HIGHEST)
    total_force = own_force + returned.reshape(tile_count, 3, TILE)
    forces = jnp.transpose(total_force, (1, 0, 2)).reshape(1, 1, 1, 3, slot_count)
    return (hidden_features.reshape(1, 1, 1, slot_count, channels), forces)


VMEM = pl.BlockSpec(memory_space=pltpu.VMEM)
SMEM = pl.BlockSpec(memory_space=pltpu.SMEM)
ANY = pl.BlockSpec(memory_space=pl.ANY)


def code_of(n):
    return n + (1 if n >= 13 else 0)


def steps_of(code):
    return (code // 9 - 1, code // 3 % 3 - 1, code % 3 - 1)


def beside(n):
    found = []
    for name, step in zip(AXES, steps_of(code_of(n))):
        place, size = lax.axis_index(name), lax.axis_size(name)
        found.append(lax.rem(place + (step + size), size) if step else place)
    return tuple(found)


def started(neighbours, source_of, target_of, send, receive):
    copies = []
    for n in range(NEAR):
        copy = pltpu.make_async_remote_copy(
            src_ref=source_of(n),
            dst_ref=target_of(NEAR - 1 - n),
            send_sem=send.at[n],
            recv_sem=receive.at[NEAR - 1 - n],
            device_id=neighbours[n],
            device_id_type=MESH,
        )
        copy.start()
        copies.append(copy)
    return copies


def finish(copies):
    for copy in copies:
        copy.wait()


def three_parts(values):
    high = values.astype(jnp.bfloat16).astype(jnp.float32)
    middle = (values - high).astype(jnp.bfloat16).astype(jnp.float32)
    low = values - high - middle
    return jnp.concatenate([high, middle, low], axis=0).astype(jnp.bfloat16)


def joined(parts):
    return parts[0:8] + parts[8:16] + parts[16:24]


def across(left, right):
    return lax.dot_general(left, right, (((1,), (1,)), ((), ())), preferred_element_type=jnp.float32)


def iota(shape, dim):
    return lax.broadcasted_iota(jnp.int32, shape, dim)


def picked_start(coords, count):
    slots = coords.shape[1]
    slot = iota((3, slots), 1)
    start = jnp.where(slot < count, coords[...], FAR_AWAY + DEAD_SPACING * slot.astype(jnp.float32))
    return jnp.concatenate([start, jnp.zeros((5, slots), jnp.float32)], axis=0)


def pair_block(with_force, pairs, chain, force_weight, rows, spots, radial, wide, edges, weighted, running, pushed, parted):
    half = iota((TILE, LANES), 1) // TILE
    within = iota((TILE, LANES), 1) % TILE
    eye = (within == iota((TILE, LANES), 0)).astype(jnp.float32)
    upper = half.astype(jnp.float32)

    def one_pair(pair, slot):
        target = pairs[0, pair]
        source = pairs[1, pair]
        before = chain[0, pair]
        same = jnp.where(target == source, 1.0, 0.0).astype(jnp.float32)
        spot = spots[source]
        gap = [wide[target, axis] - spot[axis : axis + 1, :] for axis in range(3)]
        square = gap[0] * gap[0] + gap[1] * gap[1] + gap[2] * gap[2] + SOFTENING
        inverse = lax.rsqrt(square)
        distance = square * inverse
        ramp = 1.0 - jnp.minimum(square * (1.0 / (CUTOFF * CUTOFF)), 1.0)
        envelope = ramp * ramp * (1.0 - same * eye)
        unit = [g * inverse for g in gap]
        scaled = (distance - (0.5 + STEP * upper)) * (1.0 / BASIS_WIDTH)
        root_three = math.sqrt(3.0)
        root_five = math.sqrt(5.0)
        root_fifteen = math.sqrt(15.0)
        fifteen = [root_fifteen * u for u in unit]
        angular = [
            None,
            root_three * unit[0],
            root_three * unit[1],
            root_three * unit[2],
            fifteen[0] * unit[1],
            fifteen[1] * unit[2],
            (1.5 * root_five) * unit[2] * unit[2] - 0.5 * root_five,
            fifteen[0] * unit[2],
            0.5 * (fifteen[0] * unit[0] - fifteen[1] * unit[1]),
        ]
        profile = None
        for q in range(GROUPS):
            moved = scaled - (2.0 * q * STEP / BASIS_WIDTH)
            basis = jnp.exp(-(moved * moved)) * envelope
            if with_force:
                weight = jnp.where(half == 0, force_weight[2 * q], force_weight[2 * q + 1])
                profile = weight * basis if profile is None else profile + weight * basis
            columns = slice(q * LANES, (q + 1) * LANES)
            edges[slot, 0:TILE, columns] = basis.astype(jnp.bfloat16)
            for m in range(1, 9):
                edges[slot, m * TILE : (m + 1) * TILE, columns] = (angular[m] * basis).astype(jnp.bfloat16)
        near = rows[source]
        full = near.astype(jnp.float32)
        for k in range(3 * NB):
            weighted[slot, k // NB, (k % NB) * TILE : (k % NB + 1) * TILE, :] = (
                full * radial[k : k + 1, :]
            ).astype(jnp.bfloat16)
        for order, (low, high) in enumerate(((0, 1), (1, 4), (4, 9))):
            lines = slice(low * TILE, high * TILE)
            message = multiply(edges[slot, lines, :], weighted[slot, order])
            running[pair + 1, lines, :] = message + running[before, lines, :]
        if with_force:
            twice = jnp.concatenate([near, near], axis=0)
            strength = profile * across(rows[target], twice)
            line = iota((8, LANES), 0)
            sums = jnp.zeros((8, LANES), jnp.float32)
            for axis in range(3):
                push = strength * unit[axis]
                pushed[pair + 1, axis] = push + pushed[before, axis]
                summed = jnp.sum(push, axis=0, keepdims=True)
                sums = jnp.where(line == axis, summed, sums)
            parted[pair] = sums

    def two_pairs(step, carried):
        one_pair(2 * step, 0)
        one_pair(2 * step + 1, 1)
        return carried

    count = pairs.shape[1]
    lax.fori_loop(0, count // 2, two_pairs, 0)
    for left in range(count // 2 * 2, count):
        one_pair(left, 0)


def renewed(totals, hidden, mix, out_weight):
    channels = hidden.shape[1]

    def part(m):
        return totals[m * TILE : (m + 1) * TILE, :] * MESSAGE_SCALE

    vector = part(1) ** 2 + part(2) ** 2 + part(3) ** 2
    tensor = part(4) ** 2 + part(5) ** 2 + part(6) ** 2 + part(7) ** 2 + part(8) ** 2
    mixed = mix[0:1, :] * part(0) + mix[1:2, :] * vector + mix[2:3, :] * tensor
    active = (mixed / (1.0 + jnp.exp(-mixed))).astype(jnp.bfloat16)
    return (hidden.astype(jnp.float32) + multiply(active, out_weight)).astype(jnp.bfloat16)


def step_kernel(
    edge,
    counts,
    pairs,
    force_weight,
    sources,
    wanted,
    coords,
    radial,
    mix,
    features_far,
    lift_far,
    out_weight_far,
    updated,
    forces,
    flag_out,
    block,
    lists,
    table,
    rows_sent,
    spots_sent,
    rows_came,
    spots_came,
    gathered,
    placed,
    select,
    hidden,
    own_rows,
    own_spots,
    asked_first,
    asked_last,
    asked_spots,
    near_spots,
    rows_first,
    rows_last,
    spots,
    wide,
    edges,
    weighted,
    running,
    pushed,
    parted,
    force_sent,
    force_came,
    own_force,
    lift,
    out_weight,
    fresh,
    wants,
    chain,
    local,
    send_list,
    take_list,
    send_moved,
    take_moved,
    send_spots,
    take_spots,
    send_first,
    take_first,
    send_near,
    take_near,
    send_last,
    take_last,
    send_force,
    take_force,
):
    channels = features_far.shape[1]
    slots = sources.shape[1]
    tiles = slots // TILE
    taken = NEAR * CAP
    own_base = gathered.shape[0] - slots
    neighbours = [beside(n) for n in range(NEAR)]
    barrier = pltpu.get_barrier_semaphore()
    for n in range(NEAR):
        pl.semaphore_signal(barrier, inc=1, device_id=neighbours[n], device_id_type=MESH)
    bring = [
        pltpu.make_async_copy(features_far, gathered.at[pl.ds(own_base, slots), :], local.at[0]),
        pltpu.make_async_copy(lift_far, lift, local.at[1]),
        pltpu.make_async_copy(out_weight_far, out_weight, local.at[2]),
    ]
    for copy in bring:
        copy.start()

    row_all = sources[...]
    code_row = lax.shift_right_logical(row_all, 9)
    code_row_f = code_row.astype(jnp.float32)
    level32 = iota((32, slots), 0)
    tally = jnp.sum(jnp.where(code_row == level32, 1.0, 0.0), axis=1, keepdims=True)
    tally = jnp.where(iota((32, 1), 0) == 13, 0.0, tally)
    flag = jnp.broadcast_to(
        jnp.max(jnp.where(tally > CAP, 1.0, 0.0), axis=0, keepdims=True), (1, LANES)
    )
    block[0:1, :] = row_all
    block[1:2, :] = jnp.zeros((1, slots), jnp.int32)
    for layer in range(LAYERS):
        block[1:2, 32 * layer : 32 * layer + 27] = wanted[layer : layer + 1, :]
    block[1:2, LANES : 2 * LANES] = flag.astype(jnp.int32)
    pl.semaphore_wait(barrier, NEAR)
    copies = started(neighbours, lambda n: block, lambda n: lists.at[n], send_list, take_list)

    newest = [jnp.int32(0)] * tiles
    for pair in range(pairs.shape[1]):
        target = pairs[0, pair]
        last = jnp.int32(0)
        for t in range(tiles):
            last = jnp.where(target == t, newest[t], last)
            newest[t] = jnp.where(target == t, pair + 1, newest[t])
        chain[0, pair] = last
    for t in range(tiles):
        chain[1, t] = newest[t]
    running[0] = jnp.zeros(running.shape[1:], jnp.float32)
    pushed[0] = jnp.zeros(pushed.shape[1:], jnp.float32)
    for ref in (rows_first, rows_last):
        ref[tiles + 13] = jnp.zeros(ref.shape[1:], ref.dtype)
    spots[:, tiles + 13] = jnp.zeros((2, 8, LANES), jnp.float32)
    level = iota((LANES, LANES), 0)
    lane = iota((LANES, LANES), 1)
    for first in range(slots // LANES):
        row = row_all[:, first * LANES : (first + 1) * LANES].astype(jnp.float32)
        turned = jnp.transpose(jnp.broadcast_to(row, (LANES, LANES))).astype(jnp.int32)
        code = lax.shift_right_logical(turned, 9)
        slot = jnp.bitwise_and(turned, 511)
        code_f = code.astype(jnp.float32)
        total = jnp.zeros((LANES, LANES), jnp.float32)
        for second in range(first + 1):
            same = code_f == code_row_f[:, second * LANES : (second + 1) * LANES]
            if second == first:
                same = jnp.logical_and(same, lane < level)
            total = total + jnp.where(same, 1.0, 0.0)
        rank = jnp.sum(total, axis=1, keepdims=True).astype(jnp.int32)
        neighbour = code - jnp.where(code >= 13, 1, 0)
        index = jnp.where(code == 13, own_base + slot, neighbour * CAP + rank)
        for part in range(gathered.shape[0] // LANES):
            hit = index == lane + part * LANES
            select[first * LANES : (first + 1) * LANES, part * LANES : (part + 1) * LANES] = (
                jnp.where(hit, 1.0, 0.0).astype(jnp.bfloat16)
            )
    start = picked_start(coords, counts[0])
    parts = three_parts(start)
    placed[:, 0:own_base] = jnp.zeros((8, own_base), jnp.float32)
    placed[:, own_base:] = start
    gathered[taken:own_base, :] = jnp.zeros((own_base - taken, channels), jnp.bfloat16)
    earlier = (iota((slots, slots), 0) < iota((slots, slots), 1)).astype(jnp.float32).astype(jnp.bfloat16)
    table[...] = jnp.zeros_like(table)
    spots_sent[...] = jnp.zeros_like(spots_sent)
    for copy in bring:
        copy.wait()
    finish(copies)

    fetch = pltpu.make_async_copy(lists.at[:, 1, pl.ds(0, LANES)], wants, local.at[3])
    fetch.start()
    for n in range(NEAR):
        table[n : n + 1, :] = lists[n, 0:1, :]
        flag = jnp.maximum(flag, lists[n, 1:2, LANES : 2 * LANES].astype(jnp.float32))
    held = table[...]
    number = iota(held.shape, 0)
    code = number + jnp.where(number >= 13, 1, 0)
    mine = jnp.logical_and(lax.shift_right_logical(held, 9) == 26 - code, number < NEAR)
    slot = jnp.bitwise_and(held, 511).astype(jnp.float32)
    chosen = jnp.where(mine, 1.0, 0.0)
    rank = jnp.dot(chosen.astype(jnp.bfloat16), earlier, preferred_element_type=jnp.float32)
    rank = jnp.where(mine, rank, -1.0)
    order = iota((CAP, slots), 0).astype(jnp.float32)
    across_lane = iota((CAP, slots), 1).astype(jnp.float32)
    own_features = gathered[own_base:, :]
    for n in range(NEAR):
        hit = rank[n : n + 1, :] == order
        place = jnp.sum(jnp.where(hit, slot[n : n + 1, :], 0.0), axis=1, keepdims=True)
        pick = (place == across_lane).astype(jnp.float32).astype(jnp.bfloat16)
        rows_sent[n] = jnp.dot(pick, own_features, preferred_element_type=jnp.float32).astype(jnp.bfloat16)
        spots_sent[n, :, 0:CAP] = joined(across(parts, pick))
        spots_sent[n, 7:8, :] = flag
    copies = started(
        neighbours,
        lambda n: rows_sent.at[n],
        lambda n: rows_came.at[n],
        send_moved,
        take_moved,
    ) + started(neighbours, lambda n: spots_sent.at[n], lambda n: spots_came.at[n], send_spots, take_spots)
    fetch.wait()
    finish(copies)

    gathered[0:taken, :] = rows_came[...].reshape(taken, channels)
    for n in range(NEAR):
        placed[:, n * CAP : (n + 1) * CAP] = spots_came[n, :, 0:CAP]
        flag = jnp.maximum(flag, spots_came[n, 7:8, :])
    moved = jnp.dot(select[...], gathered[...], preferred_element_type=jnp.float32).astype(jnp.bfloat16)
    hidden[...] = moved.reshape(hidden.shape)
    projected = jnp.dot(moved, lift[0], preferred_element_type=jnp.float32).astype(jnp.bfloat16)
    own_rows[...] = projected.reshape(own_rows.shape)
    position = joined(across(three_parts(placed[...]), select[...]))
    high = jnp.where(code_row >= 9, 1, 0) + jnp.where(code_row >= 18, 1, 0)
    rest = code_row - 9 * high
    middle = jnp.where(rest >= 3, 1, 0) + jnp.where(rest >= 6, 1, 0)
    low = rest - 3 * middle
    line = iota((8, slots), 0)
    shift = jnp.where(line == 0, high - 1, jnp.where(line == 1, middle - 1, low - 1))
    position = position + shift.astype(jnp.float32) * edge
    left_half = iota((8, LANES), 1) < TILE
    for t in range(tiles):
        part = position[:, t // 2 * LANES : (t // 2 + 1) * LANES]
        swapped = pltpu.roll(part, TILE, 1)
        own_spots[t] = jnp.where(left_half, part, swapped) if t % 2 == 0 else jnp.where(left_half, swapped, part)
    line8 = iota((8, LANES), 0)
    for n in range(NEAR):
        reader = 26 - code_of(n)
        asked_first[n] = own_rows[wants[n, reader]]
        near = own_spots[wants[n, reader]]
        later = pltpu.roll(own_spots[wants[n, 32 + reader]], 3, 0)
        asked_spots[n] = jnp.where(line8 < 3, near, jnp.where(line8 < 6, later, flag))
    copies = started(
        neighbours,
        lambda n: asked_first.at[n],
        lambda n: rows_first.at[tiles + code_of(n)],
        send_first,
        take_first,
    ) + started(neighbours, lambda n: asked_spots.at[n], lambda n: near_spots.at[n], send_near, take_near)
    rows_first[0:tiles] = own_rows[...]
    for t in range(tiles):
        own = own_spots[t]
        spots[0, t] = own
        spots[1, t] = own
        turned = jnp.transpose(jnp.broadcast_to(own[None], (16, 8, LANES)).reshape(LANES, LANES))
        for axis in range(3):
            wide[t, axis] = jnp.broadcast_to(turned[:TILE, axis : axis + 1], (TILE, LANES))
    finish(copies)
    for n in range(NEAR):
        code = code_of(n)
        came = near_spots[n]
        flag = jnp.maximum(flag, came[7:8, :])
        for axis, step in enumerate(steps_of(code)):
            for layer in range(2):
                where = axis + 3 * layer
                spots[layer, tiles + code, axis : axis + 1, :] = came[where : where + 1, :] + step * edge

    pair_block(
        False, pairs, chain, force_weight, rows_first, spots.at[0], radial.at[0], wide, edges, weighted, running, None, None
    )
    for t in range(tiles):
        new = renewed(running[chain[1, t]], hidden[t], mix[0], out_weight[0])
        hidden[t] = new
        later = multiply(new, lift[1]).astype(jnp.bfloat16)
        rows_last[t] = later
        own_rows[t] = later
    for n in range(NEAR):
        asked_last[n] = own_rows[wants[n, 32 + 26 - code_of(n)]]
    copies = started(
        neighbours,
        lambda n: asked_last.at[n],
        lambda n: rows_last.at[tiles + code_of(n)],
        send_last,
        take_last,
    )
    finish(copies)

    pair_block(
        True, pairs, chain, force_weight, rows_last, spots.at[1], radial.at[1], wide, edges, weighted, running, pushed, parted
    )
    factor = 0.5 / math.sqrt(channels)

    def add_part(pair, carried):
        source = pairs[1, pair]
        part = parted[pair]
        return tuple(
            held + jnp.where(source == b, part, jnp.zeros_like(part)) for b, held in enumerate(carried)
        )

    sums = lax.fori_loop(
        0,
        pairs.shape[1],
        add_part,
        tuple(jnp.zeros((8, LANES), jnp.float32) for _ in range(tiles + 27)),
    )
    sums = [(held + pltpu.roll(held, TILE, 1)) * factor for held in sums]
    for n in range(NEAR):
        force_sent[n] = jnp.where(line8 < 7, -sums[tiles + code_of(n)], flag)
    copies = started(
        neighbours, lambda n: force_sent.at[n], lambda n: force_came.at[n], send_force, take_force
    )
    lane64 = iota((TILE, LANES), 1)
    for t in range(tiles):
        fresh[t * TILE : (t + 1) * TILE, :] = renewed(running[chain[1, t]], hidden[t], mix[1], out_weight[1])
        push = pushed[chain[1, t]]
        columns = jnp.zeros((TILE, LANES), jnp.float32)
        for axis in range(3):
            columns = jnp.where(lane64 == axis, jnp.sum(push[axis], axis=1, keepdims=True), columns)
        turned = jnp.transpose(jnp.concatenate([columns, columns], axis=0))[0:8, :]
        own_force[t] = turned * factor - sums[t]
    away = pltpu.make_async_copy(fresh, updated, local.at[0])
    away.start()
    finish(copies)
    totals = [own_force[t] for t in range(tiles)]
    for n in range(NEAR):
        tile = wants[n, 32 + 26 - code_of(n)]
        came = force_came[n]
        flag = jnp.maximum(flag, came[7:8, :])
        totals = [held + jnp.where(tile == t, came, jnp.zeros_like(came)) for t, held in enumerate(totals)]
    for part in range(tiles // 2):
        both = jnp.where(left_half, totals[2 * part], totals[2 * part + 1])
        forces[:, part * LANES : (part + 1) * LANES] = both[0:3, :]
    flag_out[...] = flag.astype(jnp.int32)
    away.wait()


def body(
    features,
    coords,
    counts,
    sources,
    wanted,
    pairs,
    lifting_weight,
    radial_weight,
    mix_weight,
    out_weight,
    force_weight,
):
    slots, channels = features.shape[3], features.shape[4]
    tiles = slots // TILE
    edge = float((slots / DENSITY) ** (1.0 / 3.0))
    count = pairs.shape[4]
    held = -(-NEAR * CAP // LANES) * LANES + slots
    shape = jax.ShapeDtypeStruct
    far, bits = jnp.float32, jnp.bfloat16

    def kernel(*refs):
        step_kernel(edge, *refs)

    updated, forces, flag = pl.pallas_call(
        kernel,
        name="whole_step",
        out_shape=[
            shape((slots, channels), bits),
            shape((3, slots), far),
            shape((1, LANES), jnp.int32),
        ],
        in_specs=[SMEM] * 3 + [VMEM] * 5 + [ANY] * 3,
        out_specs=[ANY, VMEM, VMEM],
        scratch_shapes=[
            pltpu.VMEM((2, slots), jnp.int32),
            pltpu.VMEM((NEAR, 2, slots), jnp.int32),
            pltpu.VMEM((32, slots), jnp.int32),
            pltpu.VMEM((NEAR, CAP, channels), bits),
            pltpu.VMEM((NEAR, 8, LANES), far),
            pltpu.VMEM((NEAR, CAP, channels), bits),
            pltpu.VMEM((NEAR, 8, LANES), far),
            pltpu.VMEM((held, channels), bits),
            pltpu.VMEM((8, held), far),
            pltpu.VMEM((slots, held), bits),
            pltpu.VMEM((tiles, TILE, channels), bits),
            pltpu.VMEM((tiles, TILE, channels), bits),
            pltpu.VMEM((tiles, 8, LANES), far),
            pltpu.VMEM((NEAR, TILE, channels), bits),
            pltpu.VMEM((NEAR, TILE, channels), bits),
            pltpu.VMEM((NEAR, 8, LANES), far),
            pltpu.VMEM((NEAR, 8, LANES), far),
            pltpu.VMEM((tiles + 27, TILE, channels), bits),
            pltpu.VMEM((tiles + 27, TILE, channels), bits),
            pltpu.VMEM((2, tiles + 27, 8, LANES), far),
            pltpu.VMEM((tiles, 3, TILE, LANES), far),
            pltpu.VMEM((2, 9 * TILE, NB * TILE), bits),
            pltpu.VMEM((2, 3, NB * TILE, channels), bits),
            pltpu.VMEM((count + 1, 9 * TILE, channels), far),
            pltpu.VMEM((count + 1, 3, TILE, LANES), far),
            pltpu.VMEM((count, 8, LANES), far),
            pltpu.VMEM((NEAR, 8, LANES), far),
            pltpu.VMEM((NEAR, 8, LANES), far),
            pltpu.VMEM((tiles, 8, LANES), far),
            pltpu.VMEM((LAYERS, channels, channels), bits),
            pltpu.VMEM((LAYERS, channels, channels), bits),
            pltpu.VMEM((slots, channels), bits),
            pltpu.SMEM((NEAR, LANES), jnp.int32),
            pltpu.SMEM((2, LANES), jnp.int32),
            pltpu.SemaphoreType.DMA((4,)),
        ]
        + [pltpu.SemaphoreType.DMA((NEAR,))] * 14,
        compiler_params=pltpu.CompilerParams(
            collective_id=1, has_side_effects=True, vmem_limit_bytes=56 * 1024 * 1024
        ),
    )(
        counts.reshape(1),
        pairs.reshape(2, count),
        force_weight,
        sources.reshape(1, slots),
        wanted.reshape(LAYERS, 27),
        coords.reshape(3, slots),
        radial_weight.reshape(LAYERS, 3 * NB, channels),
        mix_weight,
        features.reshape(slots, channels),
        lifting_weight,
        out_weight,
    )
    updated = updated.reshape(features.shape)
    forces = forces.reshape(coords.shape)
    return lax.cond(
        flag[0, 0] > 0,
        lambda: whole_path(
            features,
            coords,
            counts,
            sources,
            wanted,
            pairs,
            lifting_weight,
            radial_weight,
            mix_weight,
            out_weight,
            force_weight,
        ),
        lambda: (updated, forces),
    )


def solution(mesh):
    placed = (
        P("gx", "gy", "gz", None, None),
        P("gx", "gy", "gz", None, None),
        P("gx", "gy", "gz"),
        P("gx", "gy", "gz", None),
        P("gx", "gy", "gz", None, None, None),
        P("gx", "gy", "gz", None, None),
        P(),
        P(),
        P(),
        P(),
        P(),
    )
    return jax.shard_map(
        body,
        mesh=mesh,
        in_specs=placed,
        out_specs=(P("gx", "gy", "gz", None, None), P("gx", "gy", "gz", None, None)),
        check_vma=False,
    )
```

```python
import math

import jax
import jax.numpy as jnp
import numpy as np
from jax import lax
from jax.experimental import pallas as pl
from jax.experimental.pallas import tpu as pltpu
from jax.sharding import PartitionSpec as P

NB = 8
TILE = 64
LAYERS = 2
PAIR_BLOCK = 2
LANES = 128
GROUPS = NB // 2
NEAR = 26
CAP = 32
AXES = ("gx", "gy", "gz")
MESH = pl.DeviceIdType.MESH

CUTOFF = 5.0
BASIS_WIDTH = 0.6
MESSAGE_SCALE = 0.2
SOFTENING = 0.25
FAR_AWAY = 1000.0
DEAD_SPACING = 100.0
DENSITY = 0.1
STEP = 4.2 / (NB - 1)


def padded(cells, sides, width):
    for axis, dim in sides:
        count = lax.axis_size(axis)
        head = lax.slice_in_dim(cells, 0, width, axis=dim)
        tail = lax.slice_in_dim(cells, cells.shape[dim] - width, cells.shape[dim], axis=dim)
        cells = jnp.concatenate(
            [
                lax.ppermute(tail, axis, [(i, (i + 1) % count) for i in range(count)]),
                cells,
                lax.ppermute(head, axis, [((i + 1) % count, i) for i in range(count)]),
            ],
            axis=dim,
        )
    return cells


def offset_table():
    return np.array(
        [
            [first_step, second_step, third_step]
            for first_step in (-1, 0, 1)
            for second_step in (-1, 0, 1)
            for third_step in (-1, 0, 1)
        ],
        dtype=np.float32,
    )


def harmonics(direction):
    along_x = direction[0]
    along_y = direction[1]
    along_z = direction[2]
    root_three = math.sqrt(3.0)
    root_five = math.sqrt(5.0)
    root_fifteen = math.sqrt(15.0)
    return jnp.stack(
        [
            jnp.ones_like(along_x),
            root_three * along_x,
            root_three * along_y,
            root_three * along_z,
            root_fifteen * along_x * along_y,
            root_fifteen * along_y * along_z,
            0.5 * root_five * (3.0 * along_z * along_z - 1.0),
            root_fifteen * along_x * along_z,
            0.5 * root_fifteen * (along_x * along_x - along_y * along_y),
        ]
    )


def multiply(left, right):
    return jnp.dot(left, right, preferred_element_type=jnp.float32)


def pair_terms(place_i, place_j, rows_i, rows_j, same_tile, radial_layer, force_weight, with_force):
    tile_size = place_i.shape[1]
    channels = rows_j.shape[1]
    wide_count = NB * tile_size
    place_wide = jnp.tile(place_j, (1, NB))
    separation = place_i[:, :, None] - place_wide[:, None, :]
    distance = jnp.sqrt(jnp.sum(separation * separation, axis=0) + SOFTENING)
    direction = separation / distance[None]
    centers = jnp.repeat(0.5 + jnp.arange(NB).astype(jnp.float32) * (4.2 / (NB - 1)), tile_size)
    ratio = jnp.minimum(distance / CUTOFF, 1.0)
    envelope = (1.0 - ratio * ratio) ** 2
    scaled = (distance - centers[None, :]) / BASIS_WIDTH
    keep_mask = 1.0 - same_tile * jnp.tile(jnp.eye(tile_size, dtype=jnp.float32), (1, NB))
    basis = jnp.exp(-scaled * scaled) * envelope * keep_mask
    angular = harmonics(direction)
    edges = (angular * basis[None]).astype(jnp.bfloat16)
    weighted = (radial_layer[:, :, None, :] * rows_j.astype(jnp.float32)[None, None]).astype(
        jnp.bfloat16
    )
    weighted = weighted.reshape(3, wide_count, channels)
    groups = ((0, 1), (1, 4), (4, 9))
    pieces = []
    for degree in range(3):
        start_row, stop_row = groups[degree]
        edge_block = edges[start_row:stop_row].reshape(
            (stop_row - start_row) * tile_size, wide_count
        )
        pieces.append(
            multiply(edge_block, weighted[degree]).reshape(
                stop_row - start_row, tile_size, channels
            )
        )
    message = jnp.concatenate(pieces, axis=0) * MESSAGE_SCALE
    if with_force:
        intersection = multiply(rows_i, rows_j.T) / math.sqrt(channels)
        basis_split = jnp.transpose(basis.reshape(tile_size, NB, tile_size), (1, 0, 2))
        profile = jnp.sum(force_weight[:, None, None] * basis_split, axis=0)
        narrow_direction = direction[:, :, :tile_size]
        pushes = (profile * intersection)[None] * narrow_direction
        return (message, 0.5 * jnp.sum(pushes, axis=2), -0.5 * jnp.sum(pushes, axis=1))
    nothing = jnp.zeros((3, tile_size), jnp.float32)
    return (message, nothing, nothing)


def update(hidden_features, totals, mix_layer, out_layer):
    channels = hidden_features.shape[1]
    scalar_part = totals[:, 0]
    vector_part = jnp.sum(totals[:, 1:4] ** 2, axis=1)
    tensor_part = jnp.sum(totals[:, 4:9] ** 2, axis=1)
    mixed = mix_layer[0] * scalar_part + mix_layer[1] * vector_part + mix_layer[2] * tensor_part
    active = jax.nn.silu(mixed).astype(jnp.bfloat16).reshape(-1, channels)
    return (hidden_features.astype(jnp.float32) + multiply(active, out_layer)).astype(jnp.bfloat16)


def opposite(grown, shape_out):
    return grown[0::2, 0::2, 0::2].reshape(shape_out)


def beside_all(placed):
    grown = padded(placed, (("gx", 0), ("gy", 1), ("gz", 2)), 1)
    return grown.reshape(27, 3, placed.shape[4])


def relay_rows(bundle):
    bundle = padded(bundle, (("gx", 0),), 1)[0::2]
    bundle = padded(bundle, (("gy", 1),), 1)[:, 0::2]
    return padded(bundle, (("gz", 2),), 1)[:, :, 0::2]


def relayed_force(bundle):
    bundle = padded(bundle, (("gx", 0),), 1)[0::2]
    bundle = padded(bundle, (("gy", 1),), 1)[:, 0::2]
    return padded(bundle, (("gz", 2),), 1)[:, :, 0::2]


def whole_path(
    features,
    coords,
    counts,
    sources,
    wanted,
    pairs,
    lifting_weight,
    radial_weight,
    mix_weight,
    out_weight,
    force_weight,
):
    slot_count = features.shape[3]
    channels = features.shape[4]
    tile_count = slot_count // TILE
    ghost_count = wanted.shape[5]
    pair_count = pairs.shape[4]
    cell_edge = (slot_count / DENSITY) ** (1.0 / 3.0)
    shifts = jnp.asarray(offset_table()) * cell_edge
    slot_index = jnp.arange(slot_count)
    dead_place = FAR_AWAY + DEAD_SPACING * slot_index.astype(jnp.float32)
    start_place = jnp.where(
        slot_index[None, :] < counts.reshape(()), coords.reshape(3, slot_count), dead_place[None, :]
    )
    anchor = sources.reshape(slot_count)
    gathered_rows = padded(features, (("gx", 0), ("gy", 1), ("gz", 2)), 1)
    hidden_features = jnp.take(gathered_rows.reshape(27 * slot_count, channels), anchor, axis=0)
    nearby_start = beside_all(start_place.reshape(1, 1, 1, 3, slot_count)) + shifts[:, :, None]
    places = jnp.take(
        jnp.transpose(nearby_start, (1, 0, 2)).reshape(3, 27 * slot_count), anchor, axis=1
    )
    nearby = beside_all(places.reshape(1, 1, 1, 3, slot_count)) + shifts[:, :, None]
    nearby_tiles = jnp.transpose(nearby.reshape(27, 3, tile_count, TILE), (0, 2, 1, 3)).reshape(
        27 * tile_count, 3, TILE
    )
    local_places = jnp.transpose(places.reshape(3, tile_count, TILE), (1, 0, 2))
    lists = wanted.reshape(LAYERS, 27, ghost_count)
    pair_list = pairs.reshape(2, pair_count)
    code_base = (jnp.arange(27) * tile_count)[:, None]
    cube_lists = jnp.transpose(lists, (1, 0, 2)).reshape(3, 3, 3, LAYERS, ghost_count)
    grown_lists = padded(cube_lists, (("gx", 0), ("gy", 1), ("gz", 2)), 1)
    requests = opposite(grown_lists, (27, LAYERS, ghost_count))
    partial_force = jnp.zeros((tile_count + 27 * ghost_count, 3, TILE), jnp.float32)
    for index_of_layer in range(LAYERS):
        projected_features = multiply(hidden_features, lifting_weight[index_of_layer]).astype(
            jnp.bfloat16
        )
        projected_tiles = projected_features.reshape(tile_count, TILE, channels)
        picked = (code_base + lists[index_of_layer]).reshape(-1)
        outgoing = jnp.take(projected_tiles, requests[:, index_of_layer].reshape(-1), axis=0)
        relayed = relay_rows(outgoing.reshape(3, 3, 3, ghost_count, TILE, channels))
        ghost_rows = relayed.reshape(27 * ghost_count, TILE, channels)
        ghost_places = jnp.take(nearby_tiles, picked, axis=0)
        source_rows = jnp.concatenate([projected_tiles, ghost_rows], axis=0)
        source_places = jnp.concatenate([local_places, ghost_places], axis=0)
        with_force = index_of_layer == LAYERS - 1
        radial_layer = radial_weight[index_of_layer]

        def pair_values(place_i, place_j, rows_i, rows_j, same_tile):
            return pair_terms(
                place_i, place_j, rows_i, rows_j, same_tile, radial_layer, force_weight, with_force
            )

        batched = jax.vmap(pair_values)

        def one_block(block_index, carried):
            totals, partial_value = carried
            targets = lax.dynamic_slice_in_dim(pair_list[0], block_index * PAIR_BLOCK, PAIR_BLOCK)
            anchors = lax.dynamic_slice_in_dim(pair_list[1], block_index * PAIR_BLOCK, PAIR_BLOCK)
            same_tile = (targets == anchors).astype(jnp.float32)
            message, on_target, on_source = batched(
                source_places[targets],
                source_places[anchors],
                source_rows[targets],
                source_rows[anchors],
                same_tile,
            )
            totals = totals.at[targets].add(message)
            partial_value = partial_value.at[targets].add(on_target).at[anchors].add(on_source)
            return (totals, partial_value)

        initial = (
            jnp.zeros((tile_count, 9, TILE, channels), jnp.float32),
            jnp.zeros((tile_count + 27 * ghost_count, 3, TILE), jnp.float32),
        )
        totals, partial_force = lax.fori_loop(0, pair_count // PAIR_BLOCK, one_block, initial)
        hidden_features = update(
            hidden_features, totals, mix_weight[index_of_layer], out_weight[index_of_layer]
        )
    own_force = partial_force[:tile_count]
    ghost_force = partial_force[tile_count:].reshape(27, ghost_count, 3 * TILE)
    tile_ids = jnp.arange(tile_count)
    arrived = relayed_force(ghost_force.reshape(3, 3, 3, ghost_count, 3 * TILE)).reshape(
        27, ghost_count, 3 * TILE
    )
    marks = (requests[:, LAYERS - 1][:, :, None] == tile_ids[None, None, :]).astype(jnp.float32)
    returned = jnp.einsum("cgt,cgx->tx", marks, arrived, precision=lax.Precision.HIGHEST)
    total_force = own_force + returned.reshape(tile_count, 3, TILE)
    forces = jnp.transpose(total_force, (1, 0, 2)).reshape(1, 1, 1, 3, slot_count)
    return (hidden_features.reshape(1, 1, 1, slot_count, channels), forces)


VMEM = pl.BlockSpec(memory_space=pltpu.VMEM)
SMEM = pl.BlockSpec(memory_space=pltpu.SMEM)
ANY = pl.BlockSpec(memory_space=pl.ANY)


CHUNK = 16
SHAPED = 1
SUMMED = 4


def code_of(n):
    return n + (1 if n >= 13 else 0)


def steps_of(code):
    return (code // 9 - 1, code // 3 % 3 - 1, code % 3 - 1)


def beside(n):
    found = []
    for name, step in zip(AXES, steps_of(code_of(n))):
        place, size = lax.axis_index(name), lax.axis_size(name)
        found.append(lax.rem(place + (step + size), size) if step else place)
    return tuple(found)


FAR_FIRST = sorted(range(NEAR), key=lambda n: -sum(abs(step) for step in steps_of(code_of(n))))


def started(neighbours, source_of, landing, first, send, receive):
    def copy_of(source, target, n):
        return pltpu.make_async_remote_copy(
            src_ref=source,
            dst_ref=target,
            send_sem=send,
            recv_sem=receive,
            device_id=neighbours[n],
            device_id_type=MESH,
        )

    for n in FAR_FIRST:
        copy_of(source_of(n), landing.at[first + NEAR - 1 - n], n).start()
    whole = landing.at[pl.ds(first, NEAR)]
    return [copy_of(whole, whole, 0)]


def finish(copies):
    for copy in copies:
        copy.wait()


def three_parts(values):
    high = values.astype(jnp.bfloat16).astype(jnp.float32)
    middle = (values - high).astype(jnp.bfloat16).astype(jnp.float32)
    low = values - high - middle
    return jnp.concatenate([high, middle, low], axis=0).astype(jnp.bfloat16)


def joined(parts):
    return parts[0:8] + parts[8:16] + parts[16:24]


def across(left, right):
    return lax.dot_general(left, right, (((1,), (1,)), ((), ())), preferred_element_type=jnp.float32)


def iota(shape, dim):
    return lax.broadcasted_iota(jnp.int32, shape, dim)


def picked_start(coords, count):
    slots = coords.shape[1] // 3
    rows = [coords[:, axis * slots : (axis + 1) * slots] for axis in range(3)]
    rows = jnp.concatenate(rows + [jnp.zeros((5, slots), jnp.float32)], axis=0)
    slot = iota((8, slots), 1)
    start = jnp.where(slot < count, rows, FAR_AWAY + DEAD_SPACING * slot.astype(jnp.float32))
    return jnp.where(iota((8, slots), 0) < 3, start, 0.0)


def row_of(source):
    return source - jnp.where(source > 21, 1, 0)


def over_pairs(count, together, one_pair):
    def some(step, carried):
        for slot in range(together):
            one_pair(step * together + slot, slot)
        return carried

    lax.fori_loop(0, count // together, some, 0)
    for left in range(count // together * together, count):
        one_pair(left, 0)


def shape_pairs(with_force, pairs, force_weight, spots, wide, edges, pull):
    half = iota((CHUNK, LANES), 1) // TILE
    within = iota((CHUNK, LANES), 1) % TILE
    level = iota((CHUNK, LANES), 0)
    upper = half.astype(jnp.float32)
    root_three = math.sqrt(3.0)
    root_five = math.sqrt(5.0)
    root_fifteen = math.sqrt(15.0)
    if with_force:
        weights = [jnp.where(half == 0, force_weight[2 * q], force_weight[2 * q + 1]) for q in range(GROUPS)]

    def one_pair(pair, slot):
        target = pairs[0, pair]
        source = pairs[1, pair]
        drop = jnp.where(target == source, 1.0, 0.0).astype(jnp.float32)
        spot = spots[row_of(source)]
        for top in range(0, TILE, CHUNK):
            lines = slice(top, top + CHUNK)
            gap = [wide[target, axis, lines, :] - spot[axis : axis + 1, :] for axis in range(3)]
            square = gap[0] * gap[0] + gap[1] * gap[1] + gap[2] * gap[2] + SOFTENING
            inverse = lax.rsqrt(square)
            ramp = 1.0 - jnp.minimum(square * (1.0 / (CUTOFF * CUTOFF)), 1.0)
            eye = jnp.where(within == level + top, drop, 0.0)
            envelope = ramp * ramp * (1.0 - eye)
            unit = [g * inverse for g in gap]
            scaled = (square * inverse) * (1.0 / BASIS_WIDTH) - (0.5 + STEP * upper) * (1.0 / BASIS_WIDTH)
            fifteen = [root_fifteen * u for u in unit]
            angular = [
                None,
                root_three * unit[0],
                root_three * unit[1],
                root_three * unit[2],
                fifteen[0] * unit[1],
                fifteen[1] * unit[2],
                (1.5 * root_five) * unit[2] * unit[2] - 0.5 * root_five,
                fifteen[0] * unit[2],
                0.5 * (fifteen[0] * unit[0] - fifteen[1] * unit[1]),
            ]
            profile = None
            for q in range(GROUPS):
                moved = scaled - (2.0 * q * STEP / BASIS_WIDTH)
                basis = jnp.exp(-(moved * moved)) * envelope
                if with_force:
                    part = weights[q] * basis
                    profile = part if profile is None else profile + part
                columns = slice(q * LANES, (q + 1) * LANES)
                edges[pair, lines, columns] = basis.astype(jnp.bfloat16)
                for m in range(1, 9):
                    edges[pair, m * TILE + top : m * TILE + top + CHUNK, columns] = (
                        angular[m] * basis
                    ).astype(jnp.bfloat16)
            if with_force:
                for axis in range(3):
                    pull[pair, axis, lines, :] = profile * unit[axis]

    over_pairs(pairs.shape[1], SHAPED, one_pair)


def sum_pairs(with_force, pairs, chain, rows, radial, edges, weighted, running, pull, pushed, parted):
    def one_pair(pair, slot):
        before = chain[0, pair]
        near = rows[row_of(pairs[1, pair])]
        full = near.astype(jnp.float32)
        for k in range(3 * NB):
            weighted[slot, k // NB, (k % NB) * TILE : (k % NB + 1) * TILE, :] = (
                full * radial[k : k + 1, :]
            ).astype(jnp.bfloat16)
        for order, (low, high) in enumerate(((0, 1), (1, 4), (4, 9))):
            lines = slice(low * TILE, high * TILE)
            message = multiply(edges[pair, lines, :], weighted[slot, order])
            running[pair + 1, lines, :] = message + running[before, lines, :]
        if with_force:
            inner = across(rows[pairs[0, pair]], jnp.concatenate([near, near], axis=0))
            line = iota((8, LANES), 0)
            sums = jnp.zeros((8, LANES), jnp.float32)
            for axis in range(3):
                push = pull[pair, axis] * inner
                pushed[pair + 1, axis] = push + pushed[before, axis]
                summed = jnp.sum(push, axis=0, keepdims=True)
                sums = jnp.where(line == axis, summed, sums)
            parted[pair] = sums

    over_pairs(pairs.shape[1], SUMMED, one_pair)


def renewed(totals, hidden, mix, out_weight):
    channels = hidden.shape[1]

    def part(m):
        return totals[m * TILE : (m + 1) * TILE, :] * MESSAGE_SCALE

    vector = part(1) ** 2 + part(2) ** 2 + part(3) ** 2
    tensor = part(4) ** 2 + part(5) ** 2 + part(6) ** 2 + part(7) ** 2 + part(8) ** 2
    mixed = mix[0:1, :] * part(0) + mix[1:2, :] * vector + mix[2:3, :] * tensor
    active = (mixed / (1.0 + jnp.exp(-mixed))).astype(jnp.bfloat16)
    return (hidden.astype(jnp.float32) + multiply(active, out_weight)).astype(jnp.bfloat16)


def step_kernel(
    edge,
    counts,
    pairs,
    force_weight,
    sources,
    wanted,
    coords,
    radial,
    mix,
    features_far,
    lift_far,
    out_weight_far,
    updated,
    forces,
    flag_out,
    block,
    lists,
    table,
    picks,
    rows_sent,
    spots_sent,
    rows_came,
    spots_came,
    gathered,
    placed,
    select,
    hidden,
    own_rows,
    own_spots,
    asked_first,
    asked_last,
    asked_spots,
    near_spots,
    rows_first,
    rows_last,
    spots,
    wide,
    edges,
    pull,
    weighted,
    running,
    pushed,
    parted,
    force_sent,
    force_came,
    own_force,
    lift,
    out_weight,
    wants,
    chain,
    local,
    send_list,
    take_list,
    send_moved,
    take_moved,
    send_spots,
    take_spots,
    send_first,
    take_first,
    send_near,
    take_near,
    send_last,
    take_last,
    send_force,
    take_force,
):
    channels = features_far.shape[1]
    slots = sources.shape[1]
    tiles = slots // TILE
    taken = NEAR * CAP
    own_base = gathered.shape[0] - slots
    neighbours = [beside(n) for n in range(NEAR)]
    barrier = pltpu.get_barrier_semaphore()
    for n in range(NEAR):
        pl.semaphore_signal(barrier, inc=1, device_id=neighbours[n], device_id_type=MESH)
    bring = [
        pltpu.make_async_copy(features_far, gathered.at[pl.ds(own_base, slots), :], local.at[0]),
        pltpu.make_async_copy(lift_far, lift, local.at[1]),
        pltpu.make_async_copy(out_weight_far, out_weight, local.at[2]),
    ]
    for copy in bring:
        copy.start()

    row_all = sources[...]
    code_row = lax.shift_right_logical(row_all, 9)
    code_row_f = code_row.astype(jnp.float32)
    level32 = iota((32, slots), 0)
    tally = jnp.sum(jnp.where(code_row == level32, 1.0, 0.0), axis=1, keepdims=True)
    tally = jnp.where(iota((32, 1), 0) == 13, 0.0, tally)
    flag = jnp.broadcast_to(
        jnp.max(jnp.where(tally > CAP, 1.0, 0.0), axis=0, keepdims=True), (1, LANES)
    )
    block[0:1, :] = row_all
    block[1:2, :] = jnp.zeros((1, slots), jnp.int32)
    for layer in range(LAYERS):
        block[1:2, 32 * layer : 32 * layer + 27] = wanted[layer : layer + 1, :]
    block[1:2, LANES : 2 * LANES] = flag.astype(jnp.int32)
    pl.semaphore_wait(barrier, NEAR)
    copies = started(neighbours, lambda n: block, lists, 0, send_list, take_list)

    newest = [jnp.int32(0)] * tiles
    for pair in range(pairs.shape[1]):
        target = pairs[0, pair]
        last = jnp.int32(0)
        for t in range(tiles):
            last = jnp.where(target == t, newest[t], last)
            newest[t] = jnp.where(target == t, pair + 1, newest[t])
        chain[0, pair] = last
    for t in range(tiles):
        chain[1, t] = newest[t]
    running[0] = jnp.zeros(running.shape[1:], jnp.float32)
    pushed[0] = jnp.zeros(pushed.shape[1:], jnp.float32)
    level = iota((LANES, LANES), 0)
    lane = iota((LANES, LANES), 1)
    for first in range(slots // LANES):
        row = row_all[:, first * LANES : (first + 1) * LANES].astype(jnp.float32)
        turned = jnp.transpose(jnp.broadcast_to(row, (LANES, LANES))).astype(jnp.int32)
        code = lax.shift_right_logical(turned, 9)
        slot = jnp.bitwise_and(turned, 511)
        code_f = code.astype(jnp.float32)
        total = jnp.zeros((LANES, LANES), jnp.float32)
        for second in range(first + 1):
            same = code_f == code_row_f[:, second * LANES : (second + 1) * LANES]
            if second == first:
                same = jnp.logical_and(same, lane < level)
            total = total + jnp.where(same, 1.0, 0.0)
        rank = jnp.sum(total, axis=1, keepdims=True).astype(jnp.int32)
        neighbour = code - jnp.where(code >= 13, 1, 0)
        index = jnp.where(code == 13, own_base + slot, neighbour * CAP + rank)
        for part in range(gathered.shape[0] // LANES):
            hit = index == lane + part * LANES
            select[first * LANES : (first + 1) * LANES, part * LANES : (part + 1) * LANES] = (
                jnp.where(hit, 1.0, 0.0).astype(jnp.bfloat16)
            )
    start = picked_start(coords, counts[0])
    parts = three_parts(start)
    placed[:, 0:own_base] = jnp.zeros((8, own_base), jnp.float32)
    placed[:, own_base:] = start
    gathered[taken:own_base, :] = jnp.zeros((own_base - taken, channels), jnp.bfloat16)
    earlier = (iota((slots, slots), 0) < iota((slots, slots), 1)).astype(jnp.float32).astype(jnp.bfloat16)
    table[...] = jnp.zeros_like(table)
    spots_sent[...] = jnp.zeros_like(spots_sent)
    for copy in bring:
        copy.wait()
    finish(copies)

    fetch = pltpu.make_async_copy(lists.at[:, 1, pl.ds(0, LANES)], wants, local.at[3])
    fetch.start()
    for n in range(NEAR):
        table[n : n + 1, :] = lists[n, 0:1, :]
        flag = jnp.maximum(flag, lists[n, 1:2, LANES : 2 * LANES].astype(jnp.float32))
    held = table[...]
    number = iota(held.shape, 0)
    code = number + jnp.where(number >= 13, 1, 0)
    mine = jnp.logical_and(lax.shift_right_logical(held, 9) == 26 - code, number < NEAR)
    slot = jnp.bitwise_and(held, 511).astype(jnp.float32)
    chosen = jnp.where(mine, 1.0, 0.0)
    rank = jnp.dot(chosen.astype(jnp.bfloat16), earlier, preferred_element_type=jnp.float32)
    rank = jnp.where(mine, rank, -1.0)
    order = iota((CAP, slots), 0).astype(jnp.float32)
    across_lane = iota((CAP, slots), 1).astype(jnp.float32)
    own_features = gathered[own_base:, :]
    for n in range(NEAR):
        hit = rank[n : n + 1, :] == order
        place = jnp.sum(jnp.where(hit, slot[n : n + 1, :], 0.0), axis=1, keepdims=True)
        picks[n * CAP : (n + 1) * CAP, :] = jnp.where(place == across_lane, 1.0, 0.0).astype(jnp.bfloat16)
    sent = jnp.dot(picks[...], own_features, preferred_element_type=jnp.float32).astype(jnp.bfloat16)
    rows_sent[...] = sent.reshape(rows_sent.shape)
    sent = joined(across(parts, picks[...]))
    for n in range(NEAR):
        spots_sent[n, :, 0:CAP] = sent[:, n * CAP : (n + 1) * CAP]
        spots_sent[n, 7:8, :] = flag
    copies = started(neighbours, lambda n: rows_sent.at[n], rows_came, 0, send_moved, take_moved)
    copies += started(neighbours, lambda n: spots_sent.at[n], spots_came, 0, send_spots, take_spots)
    fetch.wait()
    finish(copies)

    gathered[0:taken, :] = rows_came[...].reshape(taken, channels)
    for n in range(NEAR):
        placed[:, n * CAP : (n + 1) * CAP] = spots_came[n, :, 0:CAP]
        flag = jnp.maximum(flag, spots_came[n, 7:8, :])
    moved = jnp.dot(select[...], gathered[...], preferred_element_type=jnp.float32).astype(jnp.bfloat16)
    hidden[...] = moved.reshape(hidden.shape)
    projected = jnp.dot(moved, lift[0], preferred_element_type=jnp.float32).astype(jnp.bfloat16)
    own_rows[...] = projected.reshape(own_rows.shape)
    position = joined(across(three_parts(placed[...]), select[...]))
    high = jnp.where(code_row >= 9, 1, 0) + jnp.where(code_row >= 18, 1, 0)
    rest = code_row - 9 * high
    middle = jnp.where(rest >= 3, 1, 0) + jnp.where(rest >= 6, 1, 0)
    low = rest - 3 * middle
    line = iota((8, slots), 0)
    shift = jnp.where(line == 0, high - 1, jnp.where(line == 1, middle - 1, low - 1))
    position = position + shift.astype(jnp.float32) * edge
    left_half = iota((8, LANES), 1) < TILE
    for t in range(tiles):
        part = position[:, t // 2 * LANES : (t // 2 + 1) * LANES]
        swapped = pltpu.roll(part, TILE, 1)
        own_spots[t] = jnp.where(left_half, part, swapped) if t % 2 == 0 else jnp.where(left_half, swapped, part)
    line8 = iota((8, LANES), 0)
    for n in range(NEAR):
        reader = 26 - code_of(n)
        asked_first[n] = own_rows[wants[n, reader]]
        near = own_spots[wants[n, reader]]
        later = pltpu.roll(own_spots[wants[n, 32 + reader]], 3, 0)
        asked_spots[n] = jnp.where(line8 < 3, near, jnp.where(line8 < 6, later, flag))
    placing = started(neighbours, lambda n: asked_spots.at[n], near_spots, 0, send_near, take_near)
    copies = started(neighbours, lambda n: asked_first.at[n], rows_first, tiles, send_first, take_first)
    rows_first[0:tiles] = own_rows[...]
    for t in range(tiles):
        own = own_spots[t]
        spots[0, t] = own
        spots[1, t] = own
        turned = jnp.transpose(jnp.broadcast_to(own[None], (16, 8, LANES)).reshape(LANES, LANES))
        for axis in range(3):
            wide[t, axis] = jnp.broadcast_to(turned[:TILE, axis : axis + 1], (TILE, LANES))
    finish(placing)
    for n in range(NEAR):
        came = near_spots[n]
        flag = jnp.maximum(flag, came[7:8, :])
        for axis, step in enumerate(steps_of(code_of(n))):
            for layer in range(2):
                where = axis + 3 * layer
                spots[layer, tiles + n, axis : axis + 1, :] = came[where : where + 1, :] + step * edge

    shape_pairs(False, pairs, force_weight, spots.at[0], wide, edges, pull)
    finish(copies)
    sum_pairs(False, pairs, chain, rows_first, radial.at[0], edges, weighted, running, pull, pushed, parted)
    for t in range(tiles):
        new = renewed(running[chain[1, t]], hidden[t], mix[:, 0], out_weight[0])
        hidden[t] = new
        later = multiply(new, lift[1]).astype(jnp.bfloat16)
        rows_last[t] = later
        own_rows[t] = later
    for n in range(NEAR):
        asked_last[n] = own_rows[wants[n, 32 + 26 - code_of(n)]]
    copies = started(neighbours, lambda n: asked_last.at[n], rows_last, tiles, send_last, take_last)
    shape_pairs(True, pairs, force_weight, spots.at[1], wide, edges, pull)
    finish(copies)

    sum_pairs(True, pairs, chain, rows_last, radial.at[1], edges, weighted, running, pull, pushed, parted)
    factor = 0.5 / math.sqrt(channels)

    def add_part(pair, carried):
        source = pairs[1, pair]
        part = parted[pair]
        return tuple(
            held + jnp.where(source == b, part, jnp.zeros_like(part)) for b, held in enumerate(carried)
        )

    sums = lax.fori_loop(
        0,
        pairs.shape[1],
        add_part,
        tuple(jnp.zeros((8, LANES), jnp.float32) for _ in range(tiles + 27)),
    )
    sums = [(held + pltpu.roll(held, TILE, 1)) * factor for held in sums]
    for n in range(NEAR):
        force_sent[n] = jnp.where(line8 < 7, -sums[tiles + code_of(n)], flag)
    copies = started(neighbours, lambda n: force_sent.at[n], force_came, 0, send_force, take_force)
    lane64 = iota((TILE, LANES), 1)
    for t in range(tiles):
        updated[t * TILE : (t + 1) * TILE, :] = renewed(running[chain[1, t]], hidden[t], mix[:, 1], out_weight[1])
        push = pushed[chain[1, t]]
        columns = jnp.zeros((TILE, LANES), jnp.float32)
        for axis in range(3):
            columns = jnp.where(lane64 == axis, jnp.sum(push[axis], axis=1, keepdims=True), columns)
        turned = jnp.transpose(jnp.concatenate([columns, columns], axis=0))[0:8, :]
        own_force[t] = turned * factor - sums[t]
    finish(copies)
    totals = [own_force[t] for t in range(tiles)]
    for n in range(NEAR):
        tile = wants[n, 32 + 26 - code_of(n)]
        came = force_came[n]
        flag = jnp.maximum(flag, came[7:8, :])
        totals = [held + jnp.where(tile == t, came, jnp.zeros_like(came)) for t, held in enumerate(totals)]
    for part in range(tiles // 2):
        both = jnp.where(left_half, totals[2 * part], totals[2 * part + 1])
        for axis in range(3):
            column = axis * slots + part * LANES
            forces[:, column : column + LANES] = both[axis : axis + 1, :]
    flag_out[...] = flag.astype(jnp.int32)


def body(
    features,
    coords,
    counts,
    sources,
    wanted,
    pairs,
    lifting_weight,
    radial_weight,
    mix_weight,
    out_weight,
    force_weight,
):
    slots, channels = features.shape[3], features.shape[4]
    tiles = slots // TILE
    edge = float((slots / DENSITY) ** (1.0 / 3.0))
    count = pairs.shape[4]
    held = -(-NEAR * CAP // LANES) * LANES + slots
    shape = jax.ShapeDtypeStruct
    far, bits = jnp.float32, jnp.bfloat16

    def kernel(*refs):
        step_kernel(edge, *refs)

    updated, forces, flag = pl.pallas_call(
        kernel,
        name="whole_step",
        out_shape=[
            shape((slots, channels), bits),
            shape((1, 3 * slots), far),
            shape((1, LANES), jnp.int32),
        ],
        in_specs=[SMEM] * 3 + [VMEM] * 5 + [ANY] * 3,
        out_specs=[VMEM] * 3,
        scratch_shapes=[
            pltpu.VMEM((2, slots), jnp.int32),
            pltpu.VMEM((NEAR, 2, slots), jnp.int32),
            pltpu.VMEM((32, slots), jnp.int32),
            pltpu.VMEM((NEAR * CAP, slots), bits),
            pltpu.VMEM((NEAR, CAP, channels), bits),
            pltpu.VMEM((NEAR, 8, LANES), far),
            pltpu.VMEM((NEAR, CAP, channels), bits),
            pltpu.VMEM((NEAR, 8, LANES), far),
            pltpu.VMEM((held, channels), bits),
            pltpu.VMEM((8, held), far),
            pltpu.VMEM((slots, held), bits),
            pltpu.VMEM((tiles, TILE, channels), bits),
            pltpu.VMEM((tiles, TILE, channels), bits),
            pltpu.VMEM((tiles, 8, LANES), far),
            pltpu.VMEM((NEAR, TILE, channels), bits),
            pltpu.VMEM((NEAR, TILE, channels), bits),
            pltpu.VMEM((NEAR, 8, LANES), far),
            pltpu.VMEM((NEAR, 8, LANES), far),
            pltpu.VMEM((tiles + NEAR, TILE, channels), bits),
            pltpu.VMEM((tiles + NEAR, TILE, channels), bits),
            pltpu.VMEM((2, tiles + NEAR, 8, LANES), far),
            pltpu.VMEM((tiles, 3, TILE, LANES), far),
            pltpu.VMEM((count, 9 * TILE, NB * TILE), bits),
            pltpu.VMEM((count, 3, TILE, LANES), far),
            pltpu.VMEM((SUMMED, 3, NB * TILE, channels), bits),
            pltpu.VMEM((count + 1, 9 * TILE, channels), far),
            pltpu.VMEM((count + 1, 3, TILE, LANES), far),
            pltpu.VMEM((count, 8, LANES), far),
            pltpu.VMEM((NEAR, 8, LANES), far),
            pltpu.VMEM((NEAR, 8, LANES), far),
            pltpu.VMEM((tiles, 8, LANES), far),
            pltpu.VMEM((LAYERS, channels, channels), bits),
            pltpu.VMEM((LAYERS, channels, channels), bits),
            pltpu.SMEM((NEAR, LANES), jnp.int32),
            pltpu.SMEM((2, LANES), jnp.int32),
            pltpu.SemaphoreType.DMA((4,)),
        ]
        + [pltpu.SemaphoreType.DMA] * 14,
        compiler_params=pltpu.CompilerParams(
            collective_id=1, has_side_effects=True, vmem_limit_bytes=56 * 1024 * 1024
        ),
    )(
        counts.reshape(1),
        pairs.reshape(2, count),
        force_weight,
        sources.reshape(1, slots),
        wanted.reshape(LAYERS, 27),
        coords.reshape(1, 3 * slots),
        radial_weight.reshape(LAYERS, 3 * NB, channels),
        jnp.transpose(mix_weight, (1, 0, 2)),
        features.reshape(slots, channels),
        lifting_weight,
        out_weight,
    )
    updated = updated.reshape(features.shape)
    forces = forces.reshape(coords.shape)
    return lax.cond(
        flag[0, 0] > 0,
        lambda: whole_path(
            features,
            coords,
            counts,
            sources,
            wanted,
            pairs,
            lifting_weight,
            radial_weight,
            mix_weight,
            out_weight,
            force_weight,
        ),
        lambda: (updated, forces),
    )


def solution(mesh):
    placed = (
        P("gx", "gy", "gz", None, None),
        P("gx", "gy", "gz", None, None),
        P("gx", "gy", "gz"),
        P("gx", "gy", "gz", None),
        P("gx", "gy", "gz", None, None, None),
        P("gx", "gy", "gz", None, None),
        P(),
        P(),
        P(),
        P(),
        P(),
    )
    return jax.shard_map(
        body,
        mesh=mesh,
        in_specs=placed,
        out_specs=(P("gx", "gy", "gz", None, None), P("gx", "gy", "gz", None, None)),
        check_vma=False,
    )
```

```python
import math

import jax
import jax.numpy as jnp
import numpy as np
from jax import lax
from jax.experimental import pallas as pl
from jax.experimental.pallas import tpu as pltpu
from jax.sharding import PartitionSpec as P

NB = 8
TILE = 64
LAYERS = 2
PAIR_BLOCK = 2
LANES = 128
GROUPS = NB // 2
NEAR = 26
AXES = ("gx", "gy", "gz")
MESH = pl.DeviceIdType.MESH

CUTOFF = 5.0
BASIS_WIDTH = 0.6
MESSAGE_SCALE = 0.2
SOFTENING = 0.25
FAR_AWAY = 1000.0
DEAD_SPACING = 100.0
DENSITY = 0.1
STEP = 4.2 / (NB - 1)


def padded(cells, sides, width):
    for axis, dim in sides:
        count = lax.axis_size(axis)
        head = lax.slice_in_dim(cells, 0, width, axis=dim)
        tail = lax.slice_in_dim(cells, cells.shape[dim] - width, cells.shape[dim], axis=dim)
        cells = jnp.concatenate(
            [
                lax.ppermute(tail, axis, [(i, (i + 1) % count) for i in range(count)]),
                cells,
                lax.ppermute(head, axis, [((i + 1) % count, i) for i in range(count)]),
            ],
            axis=dim,
        )
    return cells


def offset_table():
    return np.array(
        [
            [first_step, second_step, third_step]
            for first_step in (-1, 0, 1)
            for second_step in (-1, 0, 1)
            for third_step in (-1, 0, 1)
        ],
        dtype=np.float32,
    )


def harmonics(direction):
    along_x = direction[0]
    along_y = direction[1]
    along_z = direction[2]
    root_three = math.sqrt(3.0)
    root_five = math.sqrt(5.0)
    root_fifteen = math.sqrt(15.0)
    return jnp.stack(
        [
            jnp.ones_like(along_x),
            root_three * along_x,
            root_three * along_y,
            root_three * along_z,
            root_fifteen * along_x * along_y,
            root_fifteen * along_y * along_z,
            0.5 * root_five * (3.0 * along_z * along_z - 1.0),
            root_fifteen * along_x * along_z,
            0.5 * root_fifteen * (along_x * along_x - along_y * along_y),
        ]
    )


def multiply(left, right):
    return jnp.dot(left, right, preferred_element_type=jnp.float32)


def pair_terms(place_i, place_j, rows_i, rows_j, same_tile, radial_layer, force_weight, with_force):
    tile_size = place_i.shape[1]
    channels = rows_j.shape[1]
    wide_count = NB * tile_size
    place_wide = jnp.tile(place_j, (1, NB))
    separation = place_i[:, :, None] - place_wide[:, None, :]
    distance = jnp.sqrt(jnp.sum(separation * separation, axis=0) + SOFTENING)
    direction = separation / distance[None]
    centers = jnp.repeat(0.5 + jnp.arange(NB).astype(jnp.float32) * (4.2 / (NB - 1)), tile_size)
    ratio = jnp.minimum(distance / CUTOFF, 1.0)
    envelope = (1.0 - ratio * ratio) ** 2
    scaled = (distance - centers[None, :]) / BASIS_WIDTH
    keep_mask = 1.0 - same_tile * jnp.tile(jnp.eye(tile_size, dtype=jnp.float32), (1, NB))
    basis = jnp.exp(-scaled * scaled) * envelope * keep_mask
    angular = harmonics(direction)
    edges = (angular * basis[None]).astype(jnp.bfloat16)
    weighted = (radial_layer[:, :, None, :] * rows_j.astype(jnp.float32)[None, None]).astype(
        jnp.bfloat16
    )
    weighted = weighted.reshape(3, wide_count, channels)
    groups = ((0, 1), (1, 4), (4, 9))
    pieces = []
    for degree in range(3):
        start_row, stop_row = groups[degree]
        edge_block = edges[start_row:stop_row].reshape(
            (stop_row - start_row) * tile_size, wide_count
        )
        pieces.append(
            multiply(edge_block, weighted[degree]).reshape(
                stop_row - start_row, tile_size, channels
            )
        )
    message = jnp.concatenate(pieces, axis=0) * MESSAGE_SCALE
    if with_force:
        intersection = multiply(rows_i, rows_j.T) / math.sqrt(channels)
        basis_split = jnp.transpose(basis.reshape(tile_size, NB, tile_size), (1, 0, 2))
        profile = jnp.sum(force_weight[:, None, None] * basis_split, axis=0)
        narrow_direction = direction[:, :, :tile_size]
        pushes = (profile * intersection)[None] * narrow_direction
        return (message, 0.5 * jnp.sum(pushes, axis=2), -0.5 * jnp.sum(pushes, axis=1))
    nothing = jnp.zeros((3, tile_size), jnp.float32)
    return (message, nothing, nothing)


def update(hidden_features, totals, mix_layer, out_layer):
    channels = hidden_features.shape[1]
    scalar_part = totals[:, 0]
    vector_part = jnp.sum(totals[:, 1:4] ** 2, axis=1)
    tensor_part = jnp.sum(totals[:, 4:9] ** 2, axis=1)
    mixed = mix_layer[0] * scalar_part + mix_layer[1] * vector_part + mix_layer[2] * tensor_part
    active = jax.nn.silu(mixed).astype(jnp.bfloat16).reshape(-1, channels)
    return (hidden_features.astype(jnp.float32) + multiply(active, out_layer)).astype(jnp.bfloat16)


def opposite(grown, shape_out):
    return grown[0::2, 0::2, 0::2].reshape(shape_out)


def beside_all(placed):
    grown = padded(placed, (("gx", 0), ("gy", 1), ("gz", 2)), 1)
    return grown.reshape(27, 3, placed.shape[4])


def relay_rows(bundle):
    bundle = padded(bundle, (("gx", 0),), 1)[0::2]
    bundle = padded(bundle, (("gy", 1),), 1)[:, 0::2]
    return padded(bundle, (("gz", 2),), 1)[:, :, 0::2]


def relayed_force(bundle):
    bundle = padded(bundle, (("gx", 0),), 1)[0::2]
    bundle = padded(bundle, (("gy", 1),), 1)[:, 0::2]
    return padded(bundle, (("gz", 2),), 1)[:, :, 0::2]


def whole_path(
    features,
    coords,
    counts,
    sources,
    wanted,
    pairs,
    lifting_weight,
    radial_weight,
    mix_weight,
    out_weight,
    force_weight,
):
    slot_count = features.shape[3]
    channels = features.shape[4]
    tile_count = slot_count // TILE
    ghost_count = wanted.shape[5]
    pair_count = pairs.shape[4]
    cell_edge = (slot_count / DENSITY) ** (1.0 / 3.0)
    shifts = jnp.asarray(offset_table()) * cell_edge
    slot_index = jnp.arange(slot_count)
    dead_place = FAR_AWAY + DEAD_SPACING * slot_index.astype(jnp.float32)
    start_place = jnp.where(
        slot_index[None, :] < counts.reshape(()), coords.reshape(3, slot_count), dead_place[None, :]
    )
    anchor = sources.reshape(slot_count)
    gathered_rows = padded(features, (("gx", 0), ("gy", 1), ("gz", 2)), 1)
    hidden_features = jnp.take(gathered_rows.reshape(27 * slot_count, channels), anchor, axis=0)
    nearby_start = beside_all(start_place.reshape(1, 1, 1, 3, slot_count)) + shifts[:, :, None]
    places = jnp.take(
        jnp.transpose(nearby_start, (1, 0, 2)).reshape(3, 27 * slot_count), anchor, axis=1
    )
    nearby = beside_all(places.reshape(1, 1, 1, 3, slot_count)) + shifts[:, :, None]
    nearby_tiles = jnp.transpose(nearby.reshape(27, 3, tile_count, TILE), (0, 2, 1, 3)).reshape(
        27 * tile_count, 3, TILE
    )
    local_places = jnp.transpose(places.reshape(3, tile_count, TILE), (1, 0, 2))
    lists = wanted.reshape(LAYERS, 27, ghost_count)
    pair_list = pairs.reshape(2, pair_count)
    code_base = (jnp.arange(27) * tile_count)[:, None]
    cube_lists = jnp.transpose(lists, (1, 0, 2)).reshape(3, 3, 3, LAYERS, ghost_count)
    grown_lists = padded(cube_lists, (("gx", 0), ("gy", 1), ("gz", 2)), 1)
    requests = opposite(grown_lists, (27, LAYERS, ghost_count))
    partial_force = jnp.zeros((tile_count + 27 * ghost_count, 3, TILE), jnp.float32)
    for index_of_layer in range(LAYERS):
        projected_features = multiply(hidden_features, lifting_weight[index_of_layer]).astype(
            jnp.bfloat16
        )
        projected_tiles = projected_features.reshape(tile_count, TILE, channels)
        picked = (code_base + lists[index_of_layer]).reshape(-1)
        outgoing = jnp.take(projected_tiles, requests[:, index_of_layer].reshape(-1), axis=0)
        relayed = relay_rows(outgoing.reshape(3, 3, 3, ghost_count, TILE, channels))
        ghost_rows = relayed.reshape(27 * ghost_count, TILE, channels)
        ghost_places = jnp.take(nearby_tiles, picked, axis=0)
        source_rows = jnp.concatenate([projected_tiles, ghost_rows], axis=0)
        source_places = jnp.concatenate([local_places, ghost_places], axis=0)
        with_force = index_of_layer == LAYERS - 1
        radial_layer = radial_weight[index_of_layer]

        def pair_values(place_i, place_j, rows_i, rows_j, same_tile):
            return pair_terms(
                place_i, place_j, rows_i, rows_j, same_tile, radial_layer, force_weight, with_force
            )

        batched = jax.vmap(pair_values)

        def one_block(block_index, carried):
            totals, partial_value = carried
            targets = lax.dynamic_slice_in_dim(pair_list[0], block_index * PAIR_BLOCK, PAIR_BLOCK)
            anchors = lax.dynamic_slice_in_dim(pair_list[1], block_index * PAIR_BLOCK, PAIR_BLOCK)
            same_tile = (targets == anchors).astype(jnp.float32)
            message, on_target, on_source = batched(
                source_places[targets],
                source_places[anchors],
                source_rows[targets],
                source_rows[anchors],
                same_tile,
            )
            totals = totals.at[targets].add(message)
            partial_value = partial_value.at[targets].add(on_target).at[anchors].add(on_source)
            return (totals, partial_value)

        initial = (
            jnp.zeros((tile_count, 9, TILE, channels), jnp.float32),
            jnp.zeros((tile_count + 27 * ghost_count, 3, TILE), jnp.float32),
        )
        totals, partial_force = lax.fori_loop(0, pair_count // PAIR_BLOCK, one_block, initial)
        hidden_features = update(
            hidden_features, totals, mix_weight[index_of_layer], out_weight[index_of_layer]
        )
    own_force = partial_force[:tile_count]
    ghost_force = partial_force[tile_count:].reshape(27, ghost_count, 3 * TILE)
    tile_ids = jnp.arange(tile_count)
    arrived = relayed_force(ghost_force.reshape(3, 3, 3, ghost_count, 3 * TILE)).reshape(
        27, ghost_count, 3 * TILE
    )
    marks = (requests[:, LAYERS - 1][:, :, None] == tile_ids[None, None, :]).astype(jnp.float32)
    returned = jnp.einsum("cgt,cgx->tx", marks, arrived, precision=lax.Precision.HIGHEST)
    total_force = own_force + returned.reshape(tile_count, 3, TILE)
    forces = jnp.transpose(total_force, (1, 0, 2)).reshape(1, 1, 1, 3, slot_count)
    return (hidden_features.reshape(1, 1, 1, slot_count, channels), forces)


VMEM = pl.BlockSpec(memory_space=pltpu.VMEM)
SMEM = pl.BlockSpec(memory_space=pltpu.SMEM)
ANY = pl.BlockSpec(memory_space=pl.ANY)


CHUNK = 16
SHAPED = 1
SUMMED = 4
PUSHED = 4


def code_of(n):
    return n + (1 if n >= 13 else 0)


def steps_of(code):
    return (code // 9 - 1, code // 3 % 3 - 1, code % 3 - 1)


def beside(n):
    found = []
    for name, step in zip(AXES, steps_of(code_of(n))):
        place, size = lax.axis_index(name), lax.axis_size(name)
        found.append(lax.rem(place + (step + size), size) if step else place)
    return tuple(found)


CAPS = [32 if sum(abs(step) for step in steps_of(code_of(n))) == 1 else 16 for n in range(NEAR)]
BASE = [sum(CAPS[:n]) for n in range(NEAR)]
TAKEN = sum(CAPS)
FACES = [n for n in range(NEAR) if CAPS[n] == 32]

FAR_FIRST = sorted(range(NEAR), key=lambda n: -sum(abs(step) for step in steps_of(code_of(n))))


def started(neighbours, source_of, target_of, whole, send, receive):
    def copy_of(source, target, n):
        return pltpu.make_async_remote_copy(
            src_ref=source,
            dst_ref=target,
            send_sem=send,
            recv_sem=receive,
            device_id=neighbours[n],
            device_id_type=MESH,
        )

    for n in FAR_FIRST:
        copy_of(source_of(n), target_of(NEAR - 1 - n), n).start()
    return [copy_of(whole, whole, 0)]


def finish(copies):
    for copy in copies:
        copy.wait()


def three_parts(values):
    high = values.astype(jnp.bfloat16).astype(jnp.float32)
    middle = (values - high).astype(jnp.bfloat16).astype(jnp.float32)
    low = values - high - middle
    return jnp.concatenate([high, middle, low], axis=0).astype(jnp.bfloat16)


def joined(parts):
    return parts[0:8] + parts[8:16] + parts[16:24]


def across(left, right):
    return lax.dot_general(left, right, (((1,), (1,)), ((), ())), preferred_element_type=jnp.float32)


def iota(shape, dim):
    return lax.broadcasted_iota(jnp.int32, shape, dim)


def picked_start(coords, count):
    slots = coords.shape[1] // 3
    rows = [coords[:, axis * slots : (axis + 1) * slots] for axis in range(3)]
    rows = jnp.concatenate(rows + [jnp.zeros((5, slots), jnp.float32)], axis=0)
    slot = iota((8, slots), 1)
    start = jnp.where(slot < count, rows, FAR_AWAY + DEAD_SPACING * slot.astype(jnp.float32))
    return jnp.where(iota((8, slots), 0) < 3, start, 0.0)


def row_of(source):
    return source - jnp.where(source > 21, 1, 0)


def over_pairs(count, together, one_pair):
    def some(step, carried):
        for slot in range(together):
            one_pair(step * together + slot, slot)
        return carried

    lax.fori_loop(0, count // together, some, 0)
    for left in range(count // together * together, count):
        one_pair(left, 0)


def shape_pairs(with_force, pairs, force_weight, spots, wide, edges, pull):
    half = iota((CHUNK, LANES), 1) // TILE
    within = iota((CHUNK, LANES), 1) % TILE
    level = iota((CHUNK, LANES), 0)
    upper = half.astype(jnp.float32)
    root_three = math.sqrt(3.0)
    root_five = math.sqrt(5.0)
    root_fifteen = math.sqrt(15.0)
    if with_force:
        weights = [jnp.where(half == 0, force_weight[2 * q], force_weight[2 * q + 1]) for q in range(GROUPS)]

    def one_pair(pair, slot):
        target = pairs[0, pair]
        source = pairs[1, pair]
        drop = jnp.where(target == source, 1.0, 0.0).astype(jnp.float32)
        spot = spots[row_of(source)]
        for top in range(0, TILE, CHUNK):
            lines = slice(top, top + CHUNK)
            gap = [wide[target, axis, lines, :] - spot[axis : axis + 1, :] for axis in range(3)]
            square = gap[0] * gap[0] + gap[1] * gap[1] + gap[2] * gap[2] + SOFTENING
            inverse = lax.rsqrt(square)
            ramp = 1.0 - jnp.minimum(square * (1.0 / (CUTOFF * CUTOFF)), 1.0)
            eye = jnp.where(within == level + top, drop, 0.0)
            envelope = ramp * ramp * (1.0 - eye)
            unit = [g * inverse for g in gap]
            scaled = (square * inverse) * (1.0 / BASIS_WIDTH) - (0.5 + STEP * upper) * (1.0 / BASIS_WIDTH)
            fifteen = [root_fifteen * u for u in unit]
            angular = [
                None,
                root_three * unit[0],
                root_three * unit[1],
                root_three * unit[2],
                fifteen[0] * unit[1],
                fifteen[1] * unit[2],
                (1.5 * root_five) * unit[2] * unit[2] - 0.5 * root_five,
                fifteen[0] * unit[2],
                0.5 * (fifteen[0] * unit[0] - fifteen[1] * unit[1]),
            ]
            profile = None
            for q in range(GROUPS):
                moved = scaled - (2.0 * q * STEP / BASIS_WIDTH)
                basis = jnp.exp(-(moved * moved)) * envelope
                if with_force:
                    part = weights[q] * basis
                    profile = part if profile is None else profile + part
                columns = slice(q * LANES, (q + 1) * LANES)
                edges[pair, lines, columns] = basis.astype(jnp.bfloat16)
                for m in range(1, 9):
                    edges[pair, m * TILE + top : m * TILE + top + CHUNK, columns] = (
                        angular[m] * basis
                    ).astype(jnp.bfloat16)
            if with_force:
                for axis in range(3):
                    pull[pair, axis, lines, :] = profile * unit[axis]

    over_pairs(pairs.shape[1], SHAPED, one_pair)


def sum_pairs(pairs, chain, rows, radial, edges, weighted, running):
    def one_pair(pair, slot):
        before = chain[0, pair]
        near = rows[row_of(pairs[1, pair])]
        full = near.astype(jnp.float32)
        for k in range(3 * NB):
            weighted[slot, k // NB, (k % NB) * TILE : (k % NB + 1) * TILE, :] = (
                full * radial[k : k + 1, :]
            ).astype(jnp.bfloat16)
        for order, (low, high) in enumerate(((0, 1), (1, 4), (4, 9))):
            lines = slice(low * TILE, high * TILE)
            message = multiply(edges[pair, lines, :], weighted[slot, order])
            running[pair + 1, lines, :] = message + running[before, lines, :]

    over_pairs(pairs.shape[1], SUMMED, one_pair)


def push_pairs(pairs, chain, rows, pull, pushed, parted):
    def one_pair(pair, slot):
        before = chain[0, pair]
        near = rows[row_of(pairs[1, pair])]
        inner = across(rows[pairs[0, pair]], jnp.concatenate([near, near], axis=0))
        line = iota((8, LANES), 0)
        sums = jnp.zeros((8, LANES), jnp.float32)
        for axis in range(3):
            push = pull[pair, axis] * inner
            pushed[pair + 1, axis] = push + pushed[before, axis]
            summed = jnp.sum(push, axis=0, keepdims=True)
            sums = jnp.where(line == axis, summed, sums)
        parted[pair + 1] = sums + parted[chain[2, pair]]

    over_pairs(pairs.shape[1], PUSHED, one_pair)


def renewed(totals, hidden, mix, out_weight):
    channels = hidden.shape[1]

    def part(m):
        return totals[m * TILE : (m + 1) * TILE, :] * MESSAGE_SCALE

    vector = part(1) ** 2 + part(2) ** 2 + part(3) ** 2
    tensor = part(4) ** 2 + part(5) ** 2 + part(6) ** 2 + part(7) ** 2 + part(8) ** 2
    mixed = mix[0:1, :] * part(0) + mix[1:2, :] * vector + mix[2:3, :] * tensor
    active = (mixed / (1.0 + jnp.exp(-mixed))).astype(jnp.bfloat16)
    return (hidden.astype(jnp.float32) + multiply(active, out_weight)).astype(jnp.bfloat16)


def step_kernel(
    edge,
    counts,
    pairs,
    force_weight,
    sources,
    wanted,
    coords,
    radial,
    mix,
    features_far,
    lift_far,
    out_weight_far,
    updated,
    forces,
    flag_out,
    block,
    lists,
    table,
    picks,
    rows_sent,
    spots_sent,
    rows_came,
    spots_came,
    gathered,
    placed,
    select,
    hidden,
    own_rows,
    own_spots,
    asked_first,
    asked_last,
    asked_spots,
    near_spots,
    rows_first,
    rows_last,
    spots,
    wide,
    edges,
    pull,
    weighted,
    running,
    pushed,
    parted,
    force_sent,
    force_came,
    own_force,
    lift,
    out_weight,
    wants,
    chain,
    local,
    send_list,
    take_list,
    send_moved,
    take_moved,
    send_spots,
    take_spots,
    send_first,
    take_first,
    send_near,
    take_near,
    send_last,
    take_last,
    send_force,
    take_force,
):
    channels = features_far.shape[1]
    slots = sources.shape[1]
    tiles = slots // TILE
    own_base = gathered.shape[0] - slots
    neighbours = [beside(n) for n in range(NEAR)]
    barrier = pltpu.get_barrier_semaphore()
    for n in range(NEAR):
        pl.semaphore_signal(barrier, inc=1, device_id=neighbours[n], device_id_type=MESH)
    bring = [
        pltpu.make_async_copy(features_far, gathered.at[pl.ds(own_base, slots), :], local.at[0]),
        pltpu.make_async_copy(lift_far, lift, local.at[1]),
        pltpu.make_async_copy(out_weight_far, out_weight, local.at[2]),
    ]
    for copy in bring:
        copy.start()

    row_all = sources[...]
    code_row = lax.shift_right_logical(row_all, 9)
    code_row_f = code_row.astype(jnp.float32)
    level32 = iota((32, slots), 0)
    tally = jnp.sum(jnp.where(code_row == level32, 1.0, 0.0), axis=1, keepdims=True)
    tally = jnp.where(iota((32, 1), 0) == 13, 0.0, tally)
    room = jnp.full((32, 1), 16.0)
    for n in FACES:
        room = jnp.where(iota((32, 1), 0) == code_of(n), 32.0, room)
    flag = jnp.broadcast_to(
        jnp.max(jnp.where(tally > room, 1.0, 0.0), axis=0, keepdims=True), (1, LANES)
    )
    block[0:1, :] = row_all
    block[1:2, :] = jnp.zeros((1, slots), jnp.int32)
    for layer in range(LAYERS):
        block[1:2, 32 * layer : 32 * layer + 27] = wanted[layer : layer + 1, :]
    block[1:2, LANES : 2 * LANES] = flag.astype(jnp.int32)
    pl.semaphore_wait(barrier, NEAR)
    copies = started(neighbours, lambda n: block, lambda n: lists.at[n], lists, send_list, take_list)

    newest = [jnp.int32(0)] * tiles
    for pair in range(pairs.shape[1]):
        target = pairs[0, pair]
        last = jnp.int32(0)
        for t in range(tiles):
            last = jnp.where(target == t, newest[t], last)
            newest[t] = jnp.where(target == t, pair + 1, newest[t])
        chain[0, pair] = last
    for t in range(tiles):
        chain[1, t] = newest[t]
    newest = [jnp.int32(0)] * (tiles + 27)
    for pair in range(pairs.shape[1]):
        source = pairs[1, pair]
        last = jnp.int32(0)
        for b in range(tiles + 27):
            last = jnp.where(source == b, newest[b], last)
            newest[b] = jnp.where(source == b, pair + 1, newest[b])
        chain[2, pair] = last
    for b in range(tiles + 27):
        chain[3, b] = newest[b]
    running[0] = jnp.zeros(running.shape[1:], jnp.float32)
    pushed[0] = jnp.zeros(pushed.shape[1:], jnp.float32)
    parted[0] = jnp.zeros(parted.shape[1:], jnp.float32)
    level = iota((LANES, LANES), 0)
    lane = iota((LANES, LANES), 1)
    for first in range(slots // LANES):
        row = row_all[:, first * LANES : (first + 1) * LANES].astype(jnp.float32)
        turned = jnp.transpose(jnp.broadcast_to(row, (LANES, LANES))).astype(jnp.int32)
        code = lax.shift_right_logical(turned, 9)
        slot = jnp.bitwise_and(turned, 511)
        code_f = code.astype(jnp.float32)
        total = jnp.zeros((LANES, LANES), jnp.float32)
        for second in range(first + 1):
            same = code_f == code_row_f[:, second * LANES : (second + 1) * LANES]
            if second == first:
                same = jnp.logical_and(same, lane < level)
            total = total + jnp.where(same, 1.0, 0.0)
        rank = jnp.sum(total, axis=1, keepdims=True).astype(jnp.int32)
        neighbour = code - jnp.where(code >= 13, 1, 0)
        base = 16 * neighbour
        for n in FACES:
            base = base + jnp.where(neighbour > n, 16, 0)
        index = jnp.where(code == 13, own_base + slot, base + rank)
        for part in range(gathered.shape[0] // LANES):
            hit = index == lane + part * LANES
            select[first * LANES : (first + 1) * LANES, part * LANES : (part + 1) * LANES] = (
                jnp.where(hit, 1.0, 0.0).astype(jnp.bfloat16)
            )
    start = picked_start(coords, counts[0])
    parts = three_parts(start)
    placed[:, 0:own_base] = jnp.zeros((8, own_base), jnp.float32)
    placed[:, own_base:] = start
    if own_base > TAKEN:
        gathered[TAKEN:own_base, :] = jnp.zeros((own_base - TAKEN, channels), jnp.bfloat16)
    earlier = (iota((slots, slots), 0) < iota((slots, slots), 1)).astype(jnp.float32).astype(jnp.bfloat16)
    table[...] = jnp.zeros_like(table)
    spots_sent[...] = jnp.zeros_like(spots_sent)
    for copy in bring:
        copy.wait()
    finish(copies)

    fetch = pltpu.make_async_copy(lists.at[:, 1, pl.ds(0, LANES)], wants, local.at[3])
    fetch.start()
    for n in range(NEAR):
        table[n : n + 1, :] = lists[n, 0:1, :]
        flag = jnp.maximum(flag, lists[n, 1:2, LANES : 2 * LANES].astype(jnp.float32))
    held = table[...]
    number = iota(held.shape, 0)
    code = number + jnp.where(number >= 13, 1, 0)
    mine = jnp.logical_and(lax.shift_right_logical(held, 9) == 26 - code, number < NEAR)
    slot = jnp.bitwise_and(held, 511).astype(jnp.float32)
    chosen = jnp.where(mine, 1.0, 0.0)
    rank = jnp.dot(chosen.astype(jnp.bfloat16), earlier, preferred_element_type=jnp.float32)
    rank = jnp.where(mine, rank, -1.0)
    order = iota((max(CAPS), slots), 0).astype(jnp.float32)
    across_lane = iota((max(CAPS), slots), 1).astype(jnp.float32)
    own_features = gathered[own_base:, :]
    for n in range(NEAR):
        hit = rank[n : n + 1, :] == order[0 : CAPS[n], :]
        place = jnp.sum(jnp.where(hit, slot[n : n + 1, :], 0.0), axis=1, keepdims=True)
        picks[BASE[n] : BASE[n] + CAPS[n], :] = jnp.where(
            place == across_lane[0 : CAPS[n], :], 1.0, 0.0
        ).astype(jnp.bfloat16)
    sent = jnp.dot(picks[...], own_features, preferred_element_type=jnp.float32).astype(jnp.bfloat16)
    rows_sent[...] = sent
    sent = joined(across(parts, picks[...]))
    for n in range(NEAR):
        spots_sent[n, :, 0 : CAPS[n]] = sent[:, BASE[n] : BASE[n] + CAPS[n]]
        spots_sent[n, 7:8, :] = flag
    copies = started(neighbours, lambda n: rows_sent.at[pl.ds(BASE[n], CAPS[n])], lambda n: rows_came.at[pl.ds(BASE[n], CAPS[n])], rows_came, send_moved, take_moved)
    copies += started(neighbours, lambda n: spots_sent.at[n], lambda n: spots_came.at[n], spots_came, send_spots, take_spots)
    fetch.wait()
    finish(copies)

    gathered[0:TAKEN, :] = rows_came[...]
    for n in range(NEAR):
        placed[:, BASE[n] : BASE[n] + CAPS[n]] = spots_came[n, :, 0 : CAPS[n]]
        flag = jnp.maximum(flag, spots_came[n, 7:8, :])
    moved = jnp.dot(select[...], gathered[...], preferred_element_type=jnp.float32).astype(jnp.bfloat16)
    hidden[...] = moved.reshape(hidden.shape)
    projected = jnp.dot(moved, lift[0], preferred_element_type=jnp.float32).astype(jnp.bfloat16)
    own_rows[...] = projected.reshape(own_rows.shape)
    position = joined(across(three_parts(placed[...]), select[...]))
    high = jnp.where(code_row >= 9, 1, 0) + jnp.where(code_row >= 18, 1, 0)
    rest = code_row - 9 * high
    middle = jnp.where(rest >= 3, 1, 0) + jnp.where(rest >= 6, 1, 0)
    low = rest - 3 * middle
    line = iota((8, slots), 0)
    shift = jnp.where(line == 0, high - 1, jnp.where(line == 1, middle - 1, low - 1))
    position = position + shift.astype(jnp.float32) * edge
    left_half = iota((8, LANES), 1) < TILE
    for t in range(tiles):
        part = position[:, t // 2 * LANES : (t // 2 + 1) * LANES]
        swapped = pltpu.roll(part, TILE, 1)
        own_spots[t] = jnp.where(left_half, part, swapped) if t % 2 == 0 else jnp.where(left_half, swapped, part)
    line8 = iota((8, LANES), 0)
    for n in range(NEAR):
        reader = 26 - code_of(n)
        asked_first[n] = own_rows[wants[n, reader]]
        near = own_spots[wants[n, reader]]
        later = pltpu.roll(own_spots[wants[n, 32 + reader]], 3, 0)
        asked_spots[n] = jnp.where(line8 < 3, near, jnp.where(line8 < 6, later, flag))
    placing = started(neighbours, lambda n: asked_spots.at[n], lambda n: near_spots.at[n], near_spots, send_near, take_near)
    copies = started(neighbours, lambda n: asked_first.at[n], lambda n: rows_first.at[tiles + n], rows_first.at[pl.ds(tiles, NEAR)], send_first, take_first)
    rows_first[0:tiles] = own_rows[...]
    for t in range(tiles):
        own = own_spots[t]
        spots[0, t] = own
        spots[1, t] = own
        turned = jnp.transpose(jnp.broadcast_to(own[None], (16, 8, LANES)).reshape(LANES, LANES))
        for axis in range(3):
            wide[t, axis] = jnp.broadcast_to(turned[:TILE, axis : axis + 1], (TILE, LANES))
    finish(placing)
    for n in range(NEAR):
        came = near_spots[n]
        flag = jnp.maximum(flag, came[7:8, :])
        for axis, step in enumerate(steps_of(code_of(n))):
            for layer in range(2):
                where = axis + 3 * layer
                spots[layer, tiles + n, axis : axis + 1, :] = came[where : where + 1, :] + step * edge

    shape_pairs(False, pairs, force_weight, spots.at[0], wide, edges, pull)
    finish(copies)
    sum_pairs(pairs, chain, rows_first, radial.at[0], edges, weighted, running)
    for t in range(tiles):
        new = renewed(running[chain[1, t]], hidden[t], mix[:, 0], out_weight[0])
        hidden[t] = new
        later = multiply(new, lift[1]).astype(jnp.bfloat16)
        rows_last[t] = later
        own_rows[t] = later
    for n in range(NEAR):
        asked_last[n] = own_rows[wants[n, 32 + 26 - code_of(n)]]
    copies = started(neighbours, lambda n: asked_last.at[n], lambda n: rows_last.at[tiles + n], rows_last.at[pl.ds(tiles, NEAR)], send_last, take_last)
    shape_pairs(True, pairs, force_weight, spots.at[1], wide, edges, pull)
    finish(copies)

    push_pairs(pairs, chain, rows_last, pull, pushed, parted)
    factor = 0.5 / math.sqrt(channels)

    def returned(b):
        held = parted[chain[3, b]]
        return (held + pltpu.roll(held, TILE, 1)) * factor

    for n in range(NEAR):
        force_sent[n] = jnp.where(line8 < 7, -returned(tiles + code_of(n)), flag)
    copies = started(neighbours, lambda n: force_sent.at[n], lambda n: force_came.at[n], force_came, send_force, take_force)
    sum_pairs(pairs, chain, rows_last, radial.at[1], edges, weighted, running)
    lane64 = iota((TILE, LANES), 1)
    for t in range(tiles):
        updated[t * TILE : (t + 1) * TILE, :] = renewed(running[chain[1, t]], hidden[t], mix[:, 1], out_weight[1])
        push = pushed[chain[1, t]]
        columns = jnp.zeros((TILE, LANES), jnp.float32)
        for axis in range(3):
            columns = jnp.where(lane64 == axis, jnp.sum(push[axis], axis=1, keepdims=True), columns)
        turned = jnp.transpose(jnp.concatenate([columns, columns], axis=0))[0:8, :]
        own_force[t] = turned * factor - returned(t)
    finish(copies)
    totals = [own_force[t] for t in range(tiles)]
    for n in range(NEAR):
        tile = wants[n, 32 + 26 - code_of(n)]
        came = force_came[n]
        flag = jnp.maximum(flag, came[7:8, :])
        totals = [held + jnp.where(tile == t, came, jnp.zeros_like(came)) for t, held in enumerate(totals)]
    for part in range(tiles // 2):
        both = jnp.where(left_half, totals[2 * part], totals[2 * part + 1])
        for axis in range(3):
            column = axis * slots + part * LANES
            forces[:, column : column + LANES] = both[axis : axis + 1, :]
    flag_out[...] = flag.astype(jnp.int32)


def body(
    features,
    coords,
    counts,
    sources,
    wanted,
    pairs,
    lifting_weight,
    radial_weight,
    mix_weight,
    out_weight,
    force_weight,
):
    slots, channels = features.shape[3], features.shape[4]
    tiles = slots // TILE
    edge = float((slots / DENSITY) ** (1.0 / 3.0))
    count = pairs.shape[4]
    held = -(-TAKEN // LANES) * LANES + slots
    shape = jax.ShapeDtypeStruct
    far, bits = jnp.float32, jnp.bfloat16

    def kernel(*refs):
        step_kernel(edge, *refs)

    updated, forces, flag = pl.pallas_call(
        kernel,
        name="whole_step",
        out_shape=[
            shape((slots, channels), bits),
            shape((1, 3 * slots), far),
            shape((1, LANES), jnp.int32),
        ],
        in_specs=[SMEM] * 3 + [VMEM] * 5 + [ANY] * 3,
        out_specs=[VMEM] * 3,
        scratch_shapes=[
            pltpu.VMEM((2, slots), jnp.int32),
            pltpu.VMEM((NEAR, 2, slots), jnp.int32),
            pltpu.VMEM((32, slots), jnp.int32),
            pltpu.VMEM((TAKEN, slots), bits),
            pltpu.VMEM((TAKEN, channels), bits),
            pltpu.VMEM((NEAR, 8, LANES), far),
            pltpu.VMEM((TAKEN, channels), bits),
            pltpu.VMEM((NEAR, 8, LANES), far),
            pltpu.VMEM((held, channels), bits),
            pltpu.VMEM((8, held), far),
            pltpu.VMEM((slots, held), bits),
            pltpu.VMEM((tiles, TILE, channels), bits),
            pltpu.VMEM((tiles, TILE, channels), bits),
            pltpu.VMEM((tiles, 8, LANES), far),
            pltpu.VMEM((NEAR, TILE, channels), bits),
            pltpu.VMEM((NEAR, TILE, channels), bits),
            pltpu.VMEM((NEAR, 8, LANES), far),
            pltpu.VMEM((NEAR, 8, LANES), far),
            pltpu.VMEM((tiles + NEAR, TILE, channels), bits),
            pltpu.VMEM((tiles + NEAR, TILE, channels), bits),
            pltpu.VMEM((2, tiles + NEAR, 8, LANES), far),
            pltpu.VMEM((tiles, 3, TILE, LANES), far),
            pltpu.VMEM((count, 9 * TILE, NB * TILE), bits),
            pltpu.VMEM((count, 3, TILE, LANES), far),
            pltpu.VMEM((SUMMED, 3, NB * TILE, channels), bits),
            pltpu.VMEM((count + 1, 9 * TILE, channels), far),
            pltpu.VMEM((count + 1, 3, TILE, LANES), far),
            pltpu.VMEM((count + 1, 8, LANES), far),
            pltpu.VMEM((NEAR, 8, LANES), far),
            pltpu.VMEM((NEAR, 8, LANES), far),
            pltpu.VMEM((tiles, 8, LANES), far),
            pltpu.VMEM((LAYERS, channels, channels), bits),
            pltpu.VMEM((LAYERS, channels, channels), bits),
            pltpu.SMEM((NEAR, LANES), jnp.int32),
            pltpu.SMEM((4, LANES), jnp.int32),
            pltpu.SemaphoreType.DMA((4,)),
        ]
        + [pltpu.SemaphoreType.DMA] * 14,
        compiler_params=pltpu.CompilerParams(
            collective_id=1, has_side_effects=True, vmem_limit_bytes=56 * 1024 * 1024
        ),
    )(
        counts.reshape(1),
        pairs.reshape(2, count),
        force_weight,
        sources.reshape(1, slots),
        wanted.reshape(LAYERS, 27),
        coords.reshape(1, 3 * slots),
        radial_weight.reshape(LAYERS, 3 * NB, channels),
        jnp.transpose(mix_weight, (1, 0, 2)),
        features.reshape(slots, channels),
        lifting_weight,
        out_weight,
    )
    updated = updated.reshape(features.shape)
    forces = forces.reshape(coords.shape)
    def settled():
        def settle(rows_in, forces_in, rows_out, forces_out):
            rows_out[...] = rows_in[...]
            forces_out[...] = forces_in[...]

        rows, pushes = pl.pallas_call(
            settle,
            name="settle",
            out_shape=[shape((slots, channels), bits), shape((1, 3 * slots), far)],
            in_specs=[VMEM] * 2,
            out_specs=[VMEM] * 2,
        )(updated.reshape(slots, channels), forces.reshape(1, 3 * slots))
        return (rows.reshape(features.shape), pushes.reshape(coords.shape))

    return lax.cond(
        flag[0, 0] > 0,
        lambda: whole_path(
            features,
            coords,
            counts,
            sources,
            wanted,
            pairs,
            lifting_weight,
            radial_weight,
            mix_weight,
            out_weight,
            force_weight,
        ),
        settled,
    )


def solution(mesh):
    placed = (
        P("gx", "gy", "gz", None, None),
        P("gx", "gy", "gz", None, None),
        P("gx", "gy", "gz"),
        P("gx", "gy", "gz", None),
        P("gx", "gy", "gz", None, None, None),
        P("gx", "gy", "gz", None, None),
        P(),
        P(),
        P(),
        P(),
        P(),
    )
    return jax.shard_map(
        body,
        mesh=mesh,
        in_specs=placed,
        out_specs=(P("gx", "gy", "gz", None, None), P("gx", "gy", "gz", None, None)),
        check_vma=False,
    )
```
